768 devices in a mesh: seq: 12 (over z_hi, x), head: 64 (over z_lo, y, core).
Axes of the slice: x: 4, y: 8, z: 12 (z_hi: 3, z_lo: 4; z = z_hi * 4 + z_lo), core: 2. Of those that a mesh axis runs over, the one named last changes fastest.
Arguments:
- query_rows: bfloat16 [24576, 64, 128], P('seq', 'head'), may hold values from -112 to 112
- key_rows: bfloat16 [24576, 64, 128], P('seq', 'head'), may hold values from -4 to 4
- value_rows: bfloat16 [24576, 64, 128], P('seq', 'head'), may hold values from -6 to 6
- attn_output: bfloat16 [24576, 64, 128], P('seq', 'head'), may hold values from -6 to 6
- out_grad: bfloat16 [24576, 4, 2048], P(('seq', 'head')), may hold values from -6 to 6
- neighbours: int32 [192, 4], replicated, may hold values from 0 to 191, as said below
- counts: int32 [192], replicated, may hold values from 2 to 128
Outputs:
- grad_query: bfloat16 [24576, 4, 2048], P(('seq', 'head'))
- grad_key: bfloat16 [24576, 4, 2048], P(('seq', 'head'))
- grad_value: bfloat16 [24576, 4, 2048], P(('seq', 'head'))
The draws below stay inside these ranges and needn't reach their ends.
Inputs may be any that keep to these rules, and one draw needn't show every extreme that they name: `neighbours`: row t lists 4 different tiles, the first being t itself, each at most half of 16 tiles away from t.
All inputs are finite; a program needn't handle non-finite values.
Results may differ from the reference program's by a relative error of at most 0.011.
Values may be sent and summed in bfloat16 or wider, within the bound.
No kernel may reach another device: no remote copies, remote signals or barrier semaphores. Data moves between devices by JAX's collectives and lax.ppermute only.
A program may use at most 64 MiB of HBM per device.

```python
import jax
import jax.numpy as jnp
from jax import lax

DH = 128
TILE = 128
NBR = 4
B = 4
TILES_DEV = 16
D = 2048
ITEMS = 64
TILES = 192
L = 24576


def paired_draw(key):
    base_key = jax.random.fold_in(key, 11)
    query_key, keys_key = jax.random.split(base_key, 2)
    query_vals = jax.random.truncated_normal(query_key, -3.9, 3.9, (L, ITEMS, DH), jnp.float32)
    key_vals = jax.random.truncated_normal(keys_key, -3.9, 3.9, (L, ITEMS, DH), jnp.float32)
    return (query_vals, key_vals)


def draw_query_rows(key, part):
    return paired_draw(key)[0].astype(jnp.bfloat16)


def draw_key_rows(key, part):
    return paired_draw(key)[1].astype(jnp.bfloat16)


def draw_neighbours(key, part):
    reach = TILES_DEV // 2
    window = 2 * reach + 1
    own_tile = jnp.arange(TILES, dtype=jnp.int32)[:, None]
    offsets = jnp.arange(window, dtype=jnp.int32)[None, :] - reach
    candidate = own_tile + offsets
    ranking = jax.random.randint(key, (TILES, window), 0, 2 ** 20, jnp.int32) * window + jnp.arange(window, dtype=jnp.int32)[None, :]
    excluded = (candidate < 0) | (candidate >= TILES) | (offsets == 0)
    ranking = jnp.where(excluded, 2 ** 30 + jnp.arange(window, dtype=jnp.int32)[None, :], ranking)
    order = jnp.argsort(ranking, axis=1, stable=True)[:, :NBR - 1]
    picked = jnp.take_along_axis(candidate, order, axis=1)
    return jnp.concatenate([own_tile, picked], axis=1).astype(jnp.int32)


def with_ends(values, stream_key, least, largest):
    longest = values.shape.index(max(values.shape))
    spots = []
    for shift in (0, 1):
        where = [jax.random.randint(jax.random.fold_in(stream_key, axis), (), 0, length) for axis, length in enumerate(values.shape)]
        where[longest] = (where[longest] + shift) % values.shape[longest]
        spots.append(tuple(where))
    return values.at[spots[0]].set(least).at[spots[1]].set(largest)


def shard_levels(key, extent, cuts, least, top_value):
    def one(dim, blocks):
        steps = jax.random.uniform(jax.random.fold_in(jax.random.fold_in(key, 6), dim), (blocks,), jnp.float32, least / len(cuts), top_value / len(cuts))
        return jnp.repeat(jnp.exp(steps), extent[dim] // blocks).reshape((-1,) + (1,) * (len(extent) - dim - 1))

    gain = one(*cuts[0])
    for cut in cuts[1:]:
        gain = gain * one(*cut)
    return gain


def centred(own_key, extent, deviation, bound, cuts=(), kind=jnp.bfloat16):
    loudness = shard_levels(own_key, extent, cuts, -0.22, 0.18) if cuts else 1.0
    drawn = jax.random.normal(own_key, extent, jnp.float32) * deviation * loudness
    return jnp.minimum(jnp.maximum(drawn, -bound), bound).astype(kind)


def setup_inputs(seed: int = 0) -> dict:
    seeds = jax.random.split(jax.random.key(seed), 8)
    return {
        "query_rows": draw_query_rows(jax.random.fold_in(seeds[7], 71), 0),
        "key_rows": draw_key_rows(jax.random.fold_in(seeds[7], 71), 0),
        "value_rows": centred(seeds[2], (L, ITEMS, DH), 1.0, 6.0, ((0, 12), (1, 64))),
        "attn_output": centred(seeds[3], (L, ITEMS, DH), 1.0, 6.0, ((0, 12), (1, 64))),
        "out_grad": centred(seeds[4], (L, B, D), 1.0, 6.0, ((0, 768),)),
        "neighbours": draw_neighbours(jax.random.fold_in(seeds[7], 71), 0),
        "counts": with_ends(jax.random.randint(seeds[6], (TILES,), 2, TILE + 1), jax.random.fold_in(seeds[6], 1), 2, TILE).astype(jnp.int32),
    }


def one_item(arrays, neighbours, key_valid, query_valid):
    query_one, key_one, value_one, output_one, grad_one = arrays
    scale_factor = DH ** -0.5
    grad_one = grad_one * query_valid[:, None].astype(grad_one.dtype)
    query_t = query_one.astype(jnp.float32).reshape(TILES, TILE, DH)
    key_t = key_one.astype(jnp.float32).reshape(TILES, TILE, DH)
    value_t = value_one.astype(jnp.float32).reshape(TILES, TILE, DH)
    output_t = output_one.astype(jnp.float32).reshape(TILES, TILE, DH)
    grad_t = grad_one.astype(jnp.float32).reshape(TILES, TILE, DH)
    key_near = key_t[neighbours]
    value_near = value_t[neighbours]
    valid_near = key_valid[neighbours]
    scores = jnp.einsum('tid,tnjd->tinj', query_t, key_near) * scale_factor
    scores = jnp.where(valid_near[:, None], scores, -jnp.inf)
    row_max = jnp.max(scores, axis=(2, 3), keepdims=True)
    log_total = row_max + jnp.log(jnp.sum(jnp.exp(scores - row_max), axis=(2, 3), keepdims=True))
    attn_probs = jnp.exp(scores - log_total)
    delta = jnp.sum(grad_t * output_t, axis=-1)
    dprobs = jnp.einsum('tid,tnjd->tinj', grad_t, value_near)
    dscore = (attn_probs * (dprobs - delta[:, :, None, None]) * scale_factor).astype(jnp.bfloat16).astype(jnp.float32)
    probs_low = attn_probs.astype(jnp.bfloat16).astype(jnp.float32)
    dquery = jnp.einsum('tinj,tnjd->tid', dscore, key_near)
    dkey_terms = jnp.einsum('tinj,tid->tnjd', dscore, query_t)
    dvalue_terms = jnp.einsum('tinj,tid->tnjd', probs_low, grad_t)
    flat_lists = neighbours.reshape(-1)
    dkey = jnp.zeros((TILES, TILE, DH), jnp.float32).at[flat_lists].add(dkey_terms.reshape(TILES * NBR, TILE, DH))
    dvalue = jnp.zeros((TILES, TILE, DH), jnp.float32).at[flat_lists].add(dvalue_terms.reshape(TILES * NBR, TILE, DH))
    return (dquery.reshape(L, DH).astype(jnp.bfloat16), dkey.reshape(L, DH).astype(jnp.bfloat16), dvalue.reshape(L, DH).astype(jnp.bfloat16))


def reference(query_rows, key_rows, value_rows, attn_output, out_grad, neighbours, counts):
    key_valid = jnp.arange(TILE, dtype=jnp.int32)[None, :] < counts[:, None]
    query_valid = key_valid.reshape(L)
    grad_items = out_grad.reshape(L, ITEMS, DH)
    stacked = tuple(jnp.moveaxis(array, 1, 0) for array in (query_rows, key_rows, value_rows, attn_output, grad_items))
    grad_q, grad_k, grad_v = lax.map(lambda arrays: one_item(arrays, neighbours, key_valid, query_valid), stacked)
    grad_query = jnp.moveaxis(grad_q, 0, 1).reshape(L, B, D)
    grad_key = jnp.moveaxis(grad_k, 0, 1).reshape(L, B, D)
    grad_value = jnp.moveaxis(grad_v, 0, 1).reshape(L, B, D)
    return (grad_query, grad_key, grad_value)
```

```python
import jax
import jax.numpy as jnp
from jax import lax
from jax.experimental import pallas as pl
from jax.experimental.pallas import tpu as pltpu
from jax.sharding import PartitionSpec as P

TILE = 128
NT = (((1,), (1,)), ((), ()))
NN = (((1,), (0,)), ((), ()))
TN = (((0,), (0,)), ((), ()))


def attend_kernel(tiles_dev, nbr_count, ring_len):
    half = tiles_dev // 2 * TILE
    own = tiles_dev * TILE

    def kernel(
        shard, nbr, cnt, q_any, k_any, v_any, o_any, g_any, klo, khi, vlo, vhi, vz,
        dq_ref, mid_k, mid_v, dk_lo, dk_hi, dv_lo, dv_hi,
        q, o, g, k_ext, v_ext, dk_acc, dv_acc, sems,
    ):
        s = shard[0]
        first_tile = s * tiles_dev
        ext_base = first_tile - tiles_dev // 2
        col = lax.rem(s, ring_len)

        def load(src, dst, i):
            pltpu.make_async_copy(src, dst, sems.at[i]).start()

        load(k_any, k_ext.at[pl.ds(half, own)], 0)
        load(v_any, v_ext.at[pl.ds(half, own)], 1)
        load(q_any, q, 2)
        load(o_any, o, 3)
        load(g_any, g, 4)
        load(klo, k_ext.at[pl.ds(0, half)], 5)
        load(khi, k_ext.at[pl.ds(half + own, half)], 6)
        v_low = v_ext.at[pl.ds(0, half)]
        v_high = v_ext.at[pl.ds(half + own, half)]

        @pl.when(col == 0)
        def _():
            load(vz, v_low, 7)

        @pl.when(col != 0)
        def _():
            load(vlo, v_low, 7)

        @pl.when(col == ring_len - 1)
        def _():
            load(vz, v_high, 8)

        @pl.when(col != ring_len - 1)
        def _():
            load(vhi, v_high, 8)

        dk_acc[...] = jnp.zeros_like(dk_acc)
        dv_acc[...] = jnp.zeros_like(dv_acc)
        for src, dst, i in (
            (k_any, k_ext.at[pl.ds(half, own)], 0),
            (v_any, v_ext.at[pl.ds(half, own)], 1),
            (q_any, q, 2),
            (o_any, o, 3),
            (g_any, g, 4),
            (klo, k_ext.at[pl.ds(0, half)], 5),
            (khi, k_ext.at[pl.ds(half + own, half)], 6),
            (vlo, v_low, 7),
            (vhi, v_high, 8),
        ):
            pltpu.make_async_copy(src, dst, sems.at[i]).wait()
        rows = lax.broadcasted_iota(jnp.int32, (TILE, TILE), 0)
        scale = TILE ** (-0.5)

        def step(t, carry):
            at = pl.ds(pl.multiple_of(t * TILE, TILE), TILE)
            tile = first_tile + t
            q_t = q[at, :]
            g_t = jnp.where(rows < cnt[tile], g[at, :].astype(jnp.float32), 0.0)
            delta = jnp.sum((g_t * o[at, :].astype(jnp.float32)).T, axis=0, keepdims=True)
            g_t = g_t.astype(jnp.bfloat16)
            places, keys, scores = [], [], []
            for n in range(nbr_count):
                near = nbr[tile * nbr_count + n]
                place = pl.ds(pl.multiple_of((near - ext_base) * TILE, TILE), TILE)
                key = k_ext[place, :]
                score = lax.dot_general(key, q_t, NT, preferred_element_type=jnp.float32) * scale
                places.append(place)
                keys.append(key)
                scores.append(jnp.where(rows < cnt[near], score, -jnp.inf))
            top = scores[0]
            for score in scores[1:]:
                top = jnp.maximum(top, score)
            top = jnp.max(top, axis=0, keepdims=True)
            probs = [jnp.exp(score - top) for score in scores]
            total = probs[0]
            for prob in probs[1:]:
                total = total + prob
            inv = 1.0 / jnp.sum(total, axis=0, keepdims=True)
            dq = jnp.zeros((TILE, TILE), jnp.float32)
            for place, key, prob in zip(places, keys, probs):
                prob = prob * inv
                dprob = lax.dot_general(
                    v_ext[place, :], g_t, NT, preferred_element_type=jnp.float32
                )
                dscore = (prob * (dprob - delta) * scale).astype(jnp.bfloat16)
                dq = dq + lax.dot_general(dscore, key, TN, preferred_element_type=jnp.float32)
                dk_acc[place, :] += lax.dot_general(
                    dscore, q_t, NN, preferred_element_type=jnp.float32
                )
                dv_acc[place, :] += lax.dot_general(
                    prob.astype(jnp.bfloat16), g_t, NN, preferred_element_type=jnp.float32
                )
            dq_ref[at, :] = dq.astype(jnp.bfloat16)
            return carry

        lax.fori_loop(0, tiles_dev, step, 0)
        mid_k[...] = dk_acc[pl.ds(half, own), :]
        mid_v[...] = dv_acc[pl.ds(half, own), :]
        dk_lo[...] = dk_acc[pl.ds(0, half), :].astype(jnp.bfloat16)
        dk_hi[...] = dk_acc[pl.ds(half + own, half), :].astype(jnp.bfloat16)
        dv_lo[...] = dv_acc[pl.ds(0, half), :].astype(jnp.bfloat16)
        dv_hi[...] = dv_acc[pl.ds(half + own, half), :].astype(jnp.bfloat16)

    return kernel


def combine_kernel(peers, share, ring_len):
    half_peers = peers // 2

    def kernel(shard, mid_k, mid_v, k_low, k_high, v_low, v_high, v_far, out):
        col = lax.rem(shard[0], ring_len)
        mk = mid_k[...].reshape(peers, share, TILE)
        mv = mid_v[...].reshape(peers, share, TILE)
        far = v_far[...]
        back = (
            (mk[:half_peers], k_low[...], 0, 0),
            (mk[half_peers:], k_high[...], 0, half_peers),
            (mv[:half_peers], jnp.where(col == 0, far, v_low[...]), 1, 0),
            (mv[half_peers:], jnp.where(col == ring_len - 1, far, v_high[...]), 1, half_peers),
        )
        for mid, term, which, start in back:
            total = mid + term.astype(jnp.float32).reshape(half_peers, share, TILE)
            out[pl.ds(start, half_peers), which] = total.astype(jnp.bfloat16)

    return kernel


def routes(seq_count, ring_len):
    rings = seq_count // ring_len
    forward = [(i, i + 1) for i in range(seq_count - 1)]
    around = [
        (r * ring_len + x, r * ring_len + (x + 1) % ring_len)
        for r in range(rings)
        for x in range(ring_len)
    ]
    across = [(r * ring_len, (r + 1) * ring_len) for r in range(rings - 1)] + [
        ((r + 1) * ring_len - 1, r * ring_len - 1) for r in range(1, rings)
    ]
    return forward, around, across


def per_device(query_rows, key_rows, value_rows, attn_output, out_grad, neighbours, counts):
    seq_rows, batch, width = out_grad.shape
    shard_tokens, _, head_dim = query_rows.shape
    nbr_count = neighbours.shape[1]
    tiles_dev = shard_tokens // TILE
    half = shard_tokens // 2
    peers = shard_tokens // seq_rows
    seq_count = lax.axis_size("seq")
    ring_len = 4 if seq_count % 4 == 0 else seq_count
    forward, around, across = routes(seq_count, ring_len)
    backward = [(b, a) for a, b in forward]
    around_back = [(b, a) for a, b in around]
    shard = lax.axis_index("seq").astype(jnp.int32)
    at_start = lax.rem(shard, ring_len) == 0

    def exchange(low, high):
        ring_low = lax.ppermute(high, "seq", around)
        ring_high = lax.ppermute(low, "seq", around_back)
        far = lax.ppermute(jnp.where(at_start, ring_low, ring_high), "seq", across)
        return ring_low, ring_high, far

    q = query_rows.reshape(shard_tokens, head_dim)
    k = key_rows.reshape(shard_tokens, head_dim)
    v = value_rows.reshape(shard_tokens, head_dim)
    o = attn_output.reshape(shard_tokens, head_dim)
    v_low, v_high, v_far = exchange(v[:half], v[half:])
    k_low = lax.ppermute(k[half:], "seq", forward)
    k_high = lax.ppermute(k[:half], "seq", backward)
    grads = lax.all_to_all(
        out_grad.reshape(seq_rows, peers, head_dim),
        "head",
        split_axis=1,
        concat_axis=0,
        tiled=True,
    ).reshape(shard_tokens, head_dim)

    smem = pl.BlockSpec(memory_space=pltpu.SMEM)
    vmem = pl.BlockSpec(memory_space=pltpu.VMEM)
    hbm = pl.BlockSpec(memory_space=pl.ANY)
    rows = jax.ShapeDtypeStruct((shard_tokens, head_dim), jnp.bfloat16)
    mid = jax.ShapeDtypeStruct((shard_tokens, head_dim), jnp.float32)
    flank = jax.ShapeDtypeStruct((half, head_dim), jnp.bfloat16)
    dq, mid_k, mid_v, dk_low, dk_high, dv_low, dv_high = pl.pallas_call(
        attend_kernel(tiles_dev, nbr_count, ring_len),
        out_shape=(rows, mid, mid, flank, flank, flank, flank),
        in_specs=[smem] * 3 + [hbm] * 10,
        out_specs=(vmem,) * 7,
        scratch_shapes=[
            pltpu.VMEM((shard_tokens, head_dim), jnp.bfloat16),
            pltpu.VMEM((shard_tokens, head_dim), jnp.bfloat16),
            pltpu.VMEM((shard_tokens, head_dim), jnp.bfloat16),
            pltpu.VMEM((2 * shard_tokens, head_dim), jnp.bfloat16),
            pltpu.VMEM((2 * shard_tokens, head_dim), jnp.bfloat16),
            pltpu.VMEM((2 * shard_tokens, head_dim), jnp.float32),
            pltpu.VMEM((2 * shard_tokens, head_dim), jnp.float32),
            pltpu.SemaphoreType.DMA((9,)),
        ],
        name="attend",
    )(
        shard.reshape(1), neighbours.reshape(-1), counts,
        q, k, v, o, grads, k_low, k_high, v_low, v_high, v_far,
    )
    rv_low, rv_high, rv_far = exchange(dv_low, dv_high)
    rk_low = lax.ppermute(dk_high, "seq", forward)
    rk_high = lax.ppermute(dk_low, "seq", backward)
    back_q = lax.all_to_all(
        dq.reshape(peers, seq_rows, head_dim), "head", split_axis=0, concat_axis=0, tiled=True
    )
    joint = pl.pallas_call(
        combine_kernel(peers, seq_rows, ring_len),
        out_shape=jax.ShapeDtypeStruct((peers, 2, seq_rows, head_dim), jnp.bfloat16),
        in_specs=[smem] + [vmem] * 7,
        out_specs=vmem,
        name="combine",
    )(shard.reshape(1), mid_k, mid_v, rk_low, rk_high, rv_low, rv_high, rv_far)
    back_kv = lax.all_to_all(joint, "head", split_axis=0, concat_axis=0, tiled=True)

    def to_rows(block):
        return block.transpose(1, 0, 2).reshape(seq_rows, batch, width)

    return to_rows(back_q), to_rows(back_kv[:, 0]), to_rows(back_kv[:, 1])


def solution(mesh):
    placed = (
        P("seq", "head", None),
        P("seq", "head", None),
        P("seq", "head", None),
        P("seq", "head", None),
        P(("seq", "head"), None, None),
        P(),
        P(),
    )
    return jax.shard_map(
        per_device,
        mesh=mesh,
        in_specs=placed,
        out_specs=(
            P(("seq", "head"), None, None),
            P(("seq", "head"), None, None),
            P(("seq", "head"), None, None),
        ),
        check_vma=False,
    )
```

```python
import math

import jax
import jax.numpy as jnp
from jax import lax
from jax.experimental import pallas as pl
from jax.experimental.pallas import tpu as pltpu
from jax.sharding import PartitionSpec as P

TILE = 128
NT = (((1,), (1,)), ((), ()))
NN = (((1,), (0,)), ((), ()))
TN = (((0,), (0,)), ((), ()))


def dot(a, b, dims):
    return lax.dot_general(a, b, dims, preferred_element_type=jnp.float32)


def own_kernel(tiles_dev, nbr_count, ring_len):
    half_tiles = tiles_dev // 2
    half = half_tiles * TILE
    own = tiles_dev * TILE
    scale = TILE ** (-0.5)
    scale_two = scale * math.log2(math.e)

    def kernel(
        shard, nbr, cnt, q_any, k_any, v_any, o_any, g_any, klo, khi, vlo, vhi, vz,
        dq_ref, dk_ref, dv_ref, stat_lo, stat_hi,
        q, o, g, k_ext, v_ext, dk_acc, dv_acc, stats, p_even, p_odd, sems,
    ):
        s = shard[0]
        first_tile = s * tiles_dev
        ext_base = first_tile - half_tiles
        col = lax.rem(s, ring_len)
        v_low = v_ext.at[pl.ds(0, half)]
        v_high = v_ext.at[pl.ds(half + own, half)]
        moves = [
            (k_any, k_ext.at[pl.ds(half, own)]),
            (v_any, v_ext.at[pl.ds(half, own)]),
            (q_any, q),
            (o_any, o),
            (g_any, g),
            (klo, k_ext.at[pl.ds(0, half)]),
            (khi, k_ext.at[pl.ds(half + own, half)]),
            (vlo, v_low),
            (vhi, v_high),
        ]

        def load(i, src=None):
            source = moves[i][0] if src is None else src
            pltpu.make_async_copy(source, moves[i][1], sems.at[i]).start()

        for i in range(7):
            load(i)
        pl.when(col == 0)(lambda: load(7, vz))
        pl.when(col != 0)(lambda: load(7))
        pl.when(col == ring_len - 1)(lambda: load(8, vz))
        pl.when(col != ring_len - 1)(lambda: load(8))
        dk_acc[pl.ds(0, own), :] = jnp.zeros((own, TILE), jnp.float32)
        dv_acc[pl.ds(0, own), :] = jnp.zeros((own, TILE), jnp.float32)
        for i, (src, dst) in enumerate(moves):
            pltpu.make_async_copy(src, dst, sems.at[i]).wait()
        rows = lax.broadcasted_iota(jnp.int32, (TILE, TILE), 0)

        def span(t):
            return pl.ds(pl.multiple_of(t * TILE, TILE), TILE)

        def scores(t, p_ref):
            tile = first_tile + t
            q_t = q[span(t), :]
            top = None
            for n in range(nbr_count):
                near = nbr[tile * nbr_count + n]
                key = k_ext[span(near - ext_base), :]
                score = dot(key, q_t, NT) * scale_two
                score = jnp.where(rows < cnt[near], score, -jnp.inf)
                p_ref[n] = score
                peak = jnp.max(score, axis=0, keepdims=True)
                top = peak if top is None else jnp.maximum(top, peak)
            total = jnp.zeros((1, TILE), jnp.float32)
            for n in range(nbr_count):
                prob = jnp.exp2(p_ref[n] - top)
                p_ref[n] = prob
                total = total + jnp.sum(prob, axis=0, keepdims=True)
            stats[pl.ds(t, 1), :] = top + jnp.log2(total)
            stats[pl.ds(2 * tiles_dev + t, 1), :] = 1.0 / total

        def grads(t, p_ref):
            tile = first_tile + t
            at = span(t)
            q_t = q[at, :]
            g_t = jnp.where(rows < cnt[tile], g[at, :].astype(jnp.float32), 0.0)
            delta = jnp.sum((g_t * o[at, :].astype(jnp.float32)).T, axis=0, keepdims=True)
            stats[pl.ds(tiles_dev + t, 1), :] = delta
            inv = stats[pl.ds(2 * tiles_dev + t, 1), :]
            g_t = g_t.astype(jnp.bfloat16)
            dq = None
            for n in range(nbr_count):
                place = nbr[tile * nbr_count + n] - ext_base
                mine = place - half_tiles
                mine = jnp.where((mine >= 0) & (mine < tiles_dev), mine, tiles_dev)
                prob = p_ref[n] * inv
                dprob = dot(v_ext[span(place), :], g_t, NT)
                dscore = (prob * (dprob - delta) * scale).astype(jnp.bfloat16)
                term = dot(dscore, k_ext[span(place), :], TN)
                dq = term if dq is None else dq + term
                dk_acc[span(mine), :] += dot(dscore, q_t, NN)
                dv_acc[span(mine), :] += dot(prob.astype(jnp.bfloat16), g_t, NN)
            dq_ref[at, :] = dq.astype(jnp.bfloat16)

        scores(0, p_even)

        def step(i, carry):
            t = 2 * i
            scores(t + 1, p_odd)
            grads(t, p_even)
            scores(jnp.minimum(t + 2, tiles_dev - 1), p_even)
            grads(t + 1, p_odd)
            return carry

        lax.fori_loop(0, tiles_dev // 2, step, 0)
        dk_ref[...] = dk_acc[pl.ds(0, own), :]
        dv_ref[...] = dv_acc[pl.ds(0, own), :]
        stat_lo[pl.ds(0, half_tiles), :] = stats[pl.ds(0, half_tiles), :]
        stat_lo[pl.ds(half_tiles, half_tiles), :] = stats[pl.ds(tiles_dev, half_tiles), :]
        stat_hi[pl.ds(0, half_tiles), :] = stats[pl.ds(half_tiles, half_tiles), :]
        stat_hi[pl.ds(half_tiles, half_tiles), :] = stats[
            pl.ds(tiles_dev + half_tiles, half_tiles), :
        ]

    return kernel


def near_kernel(tiles_dev, tiles_all, nbr_count, ring_len, peers):
    half_tiles = tiles_dev // 2
    half = half_tiles * TILE
    own = tiles_dev * TILE
    share = own // peers
    scale = TILE ** (-0.5)
    scale_two = scale * math.log2(math.e)

    def kernel(
        shard, nbr, cnt, k_any, v_any, dk_any, dv_any, slo, shi, glo, ghi, qlo, qhi, qz,
        joint, k, v, dk_acc, dv_acc, q, g, stats, pairs, sems,
    ):
        s = shard[0]
        first_tile = s * tiles_dev
        col = lax.rem(s, ring_len)
        q_low = q.at[pl.ds(0, half)]
        q_high = q.at[pl.ds(half, half)]
        moves = [
            (k_any, k),
            (v_any, v),
            (dk_any, dk_acc.at[pl.ds(0, own)]),
            (dv_any, dv_acc.at[pl.ds(0, own)]),
            (slo, stats.at[0]),
            (shi, stats.at[1]),
            (glo, g.at[pl.ds(0, half)]),
            (ghi, g.at[pl.ds(half, half)]),
            (qlo, q_low),
            (qhi, q_high),
        ]

        def load(i, src=None):
            source = moves[i][0] if src is None else src
            pltpu.make_async_copy(source, moves[i][1], sems.at[i]).start()

        for i in range(8):
            load(i)
        pl.when(col == 0)(lambda: load(8, qz))
        pl.when(col != 0)(lambda: load(8))
        pl.when(col == ring_len - 1)(lambda: load(9, qz))
        pl.when(col != ring_len - 1)(lambda: load(9))

        def scan(i, count):
            tile = jnp.where(
                i < half_tiles, first_tile - half_tiles + i, first_tile + tiles_dev + i - half_tiles
            )
            inside = (tile >= 0) & (tile < tiles_all)
            safe = jnp.where(inside, tile, 0)
            for n in range(1, nbr_count):
                mine = nbr[safe * nbr_count + n] - first_tile
                hit = inside & (mine >= 0) & (mine < tiles_dev)
                pairs[0, count] = i
                pairs[1, count] = mine
                count = count + hit.astype(jnp.int32)
            return count

        count = lax.fori_loop(0, tiles_dev, scan, jnp.int32(0))
        pairs[0, count] = 0
        pairs[1, count] = tiles_dev
        for i, (src, dst) in enumerate(moves):
            pltpu.make_async_copy(src, dst, sems.at[i]).wait()
        rows = lax.broadcasted_iota(jnp.int32, (TILE, TILE), 0)

        def span(t):
            return pl.ds(pl.multiple_of(t * TILE, TILE), TILE)

        def terms(index):
            i = pairs[0, index]
            mine = pairs[1, index]
            read = jnp.minimum(mine, tiles_dev - 1)
            side = jnp.where(i < half_tiles, 0, 1)
            line = i - side * half_tiles
            tile = first_tile + jnp.where(side == 0, i - half_tiles, tiles_dev + line)
            q_t = q[span(i), :]
            held = cnt[jnp.clip(tile, 0, tiles_all - 1)]
            g_t = jnp.where(rows < held, g[span(i), :].astype(jnp.float32), 0.0)
            g_t = g_t.astype(jnp.bfloat16)
            log_row = stats[side, pl.ds(line, 1), :]
            delta = stats[side, pl.ds(half_tiles + line, 1), :]
            score = dot(k[span(read), :], q_t, NT) * scale_two
            score = jnp.where(rows < cnt[first_tile + read], score - log_row, -jnp.inf)
            prob = jnp.exp2(score)
            dprob = dot(v[span(read), :], g_t, NT)
            dscore = (prob * (dprob - delta) * scale).astype(jnp.bfloat16)
            return mine, dot(dscore, q_t, NN), dot(prob.astype(jnp.bfloat16), g_t, NN)

        def step(j, carry):
            first = terms(2 * j)
            second = terms(2 * j + 1)
            for mine, dk, dv in (first, second):
                dk_acc[span(mine), :] += dk
                dv_acc[span(mine), :] += dv
            return carry

        lax.fori_loop(0, (count + 1) // 2, step, 0)
        for which, acc in ((0, dk_acc), (1, dv_acc)):
            joint[:, which] = (
                acc[pl.ds(0, own), :].astype(jnp.bfloat16).reshape(peers, share, TILE)
            )

    return kernel


def routes(seq_count, ring_len):
    rings = seq_count // ring_len
    forward = [(i, i + 1) for i in range(seq_count - 1)]
    around = [
        (r * ring_len + x, r * ring_len + (x + 1) % ring_len)
        for r in range(rings)
        for x in range(ring_len)
    ]
    across = [(r * ring_len, (r + 1) * ring_len) for r in range(rings - 1)] + [
        ((r + 1) * ring_len - 1, r * ring_len - 1) for r in range(1, rings)
    ]
    return forward, around, across


def device_work(query_rows, key_rows, value_rows, attn_output, out_grad, neighbours, counts):
    seq_rows, batch, width = out_grad.shape
    shard_tokens, _, head_dim = query_rows.shape
    nbr_count = neighbours.shape[1]
    tiles_all = counts.shape[0]
    tiles_dev = shard_tokens // TILE
    half = shard_tokens // 2
    peers = shard_tokens // seq_rows
    seq_count = lax.axis_size("seq")
    ring_len = 4 if seq_count % 4 == 0 else seq_count
    forward, around, across = routes(seq_count, ring_len)
    backward = [(b, a) for a, b in forward]
    around_back = [(b, a) for a, b in around]
    shard = lax.axis_index("seq").astype(jnp.int32)
    at_start = lax.rem(shard, ring_len) == 0

    def ring(rows):
        return (
            lax.ppermute(rows[half:], "seq", around),
            lax.ppermute(rows[:half], "seq", around_back),
        )

    def cross(low, high):
        return lax.ppermute(jnp.where(at_start, low, high), "seq", across)

    def direct(low, high):
        return lax.ppermute(high, "seq", forward), lax.ppermute(low, "seq", backward)

    q = query_rows.reshape(shard_tokens, head_dim)
    k = key_rows.reshape(shard_tokens, head_dim)
    v = value_rows.reshape(shard_tokens, head_dim)
    o = attn_output.reshape(shard_tokens, head_dim)
    table = neighbours.reshape(-1)
    v_low, v_high = ring(v)
    k_low, k_high = direct(k[:half], k[half:])
    v_far = cross(v_low, v_high)
    sent = out_grad.reshape(seq_rows, peers, head_dim).transpose(1, 0, 2)
    grads = lax.all_to_all(sent, "head", split_axis=0, concat_axis=0, tiled=True)
    grads = grads.reshape(shard_tokens, head_dim)
    q_late, v_low, v_high = lax.optimization_barrier((q, v_low, v_high))
    q_low, q_high = ring(q_late)
    g_low, g_high = direct(grads[:half], grads[half:])
    q_low, q_high, v_far = lax.optimization_barrier((q_low, q_high, v_far))
    q_far = cross(q_low, q_high)

    smem = pl.BlockSpec(memory_space=pltpu.SMEM)
    vmem = pl.BlockSpec(memory_space=pltpu.VMEM)
    hbm = pl.BlockSpec(memory_space=pl.ANY)
    rows = jax.ShapeDtypeStruct((shard_tokens, head_dim), jnp.bfloat16)
    sums = jax.ShapeDtypeStruct((shard_tokens, head_dim), jnp.float32)
    stat = jax.ShapeDtypeStruct((tiles_dev, head_dim), jnp.float32)
    held = pltpu.VMEM((shard_tokens, head_dim), jnp.bfloat16)
    wide = pltpu.VMEM((2 * shard_tokens, head_dim), jnp.bfloat16)
    acc = pltpu.VMEM((shard_tokens + TILE, head_dim), jnp.float32)
    tile_probs = pltpu.VMEM((nbr_count, TILE, TILE), jnp.float32)
    dq, dk, dv, stat_low, stat_high = pl.pallas_call(
        own_kernel(tiles_dev, nbr_count, ring_len),
        out_shape=(rows, sums, sums, stat, stat),
        in_specs=[smem] * 3 + [hbm] * 10,
        out_specs=(vmem,) * 5,
        scratch_shapes=[
            held, held, held, wide, wide, acc, acc,
            pltpu.VMEM((3 * tiles_dev, head_dim), jnp.float32),
            tile_probs, tile_probs,
            pltpu.SemaphoreType.DMA((9,)),
        ],
        name="own",
    )(shard.reshape(1), table, counts, q, k, v, o, grads, k_low, k_high, v_low, v_high, v_far)
    stat_low, stat_high = direct(stat_low, stat_high)
    back_q = lax.all_to_all(
        dq.reshape(peers, seq_rows, head_dim), "head", split_axis=0, concat_axis=0, tiled=True
    )
    joint = pl.pallas_call(
        near_kernel(tiles_dev, tiles_all, nbr_count, ring_len, peers),
        out_shape=jax.ShapeDtypeStruct((peers, 2, seq_rows, head_dim), jnp.bfloat16),
        in_specs=[smem] * 3 + [hbm] * 11,
        out_specs=vmem,
        scratch_shapes=[
            held, held, acc, acc, held, held,
            pltpu.VMEM((2, tiles_dev, head_dim), jnp.float32),
            pltpu.SMEM((2, tiles_dev * nbr_count), jnp.int32),
            pltpu.SemaphoreType.DMA((10,)),
        ],
        name="near",
    )(
        shard.reshape(1), table, counts, k, v, dk, dv,
        stat_low, stat_high, g_low, g_high, q_low, q_high, q_far,
    )
    back_kv = lax.all_to_all(joint, "head", split_axis=0, concat_axis=0, tiled=True)

    def to_rows(block):
        return block.transpose(1, 0, 2).reshape(seq_rows, batch, width)

    return to_rows(back_q), to_rows(back_kv[:, 0]), to_rows(back_kv[:, 1])


def solution(mesh):
    placed = (
        P("seq", "head", None),
        P("seq", "head", None),
        P("seq", "head", None),
        P("seq", "head", None),
        P(("seq", "head"), None, None),
        P(),
        P(),
    )
    return jax.shard_map(
        device_work,
        mesh=mesh,
        in_specs=placed,
        out_specs=(
            P(("seq", "head"), None, None),
            P(("seq", "head"), None, None),
            P(("seq", "head"), None, None),
        ),
        check_vma=False,
    )
```

```python
import math

import jax
import jax.numpy as jnp
from jax import lax
from jax.experimental import pallas as pl
from jax.experimental.pallas import tpu as pltpu
from jax.sharding import PartitionSpec as P

TILE = 128
NT = (((1,), (1,)), ((), ()))
NN = (((1,), (0,)), ((), ()))
TN = (((0,), (0,)), ((), ()))


def dot(a, b, dims):
    return lax.dot_general(a, b, dims, preferred_element_type=jnp.float32)


def span(t):
    return pl.ds(pl.multiple_of(t * TILE, TILE), TILE)


def start_copies(moves, sems):
    for i, (dst, choice) in enumerate(moves):
        if len(choice) == 1:
            pltpu.make_async_copy(choice[0], dst, sems.at[i]).start()
        else:
            far, use_far, near = choice

            @pl.when(use_far)
            def _():
                pltpu.make_async_copy(far, dst, sems.at[i]).start()

            @pl.when(jnp.logical_not(use_far))
            def _():
                pltpu.make_async_copy(near, dst, sems.at[i]).start()


def wait_copies(moves, sems):
    for i, (dst, choice) in enumerate(moves):
        pltpu.make_async_copy(choice[-1], dst, sems.at[i]).wait()


def stats_kernel(tiles_dev, nbr_count, ring_len):
    half_tiles = tiles_dev // 2
    half = half_tiles * TILE
    own = tiles_dev * TILE
    scale_two = TILE ** (-0.5) * math.log2(math.e)

    def kernel(
        shard, nbr, cnt, q_any, k_any, o_any, g_any, kv_lo, kv_hi, kz,
        stat_all, stat_lo, stat_hi,
        q, o, g, k_ext, sems,
    ):
        s = shard[0]
        first_tile = s * tiles_dev
        ext_base = first_tile - half_tiles
        col = lax.rem(s, ring_len)
        moves = (
            (k_ext.at[pl.ds(half, own)], (k_any,)),
            (q, (q_any,)),
            (o, (o_any,)),
            (g, (g_any,)),
            (k_ext.at[pl.ds(0, half)], (kz, col == 0, kv_lo.at[pl.ds(0, half)])),
            (
                k_ext.at[pl.ds(half + own, half)],
                (kz, col == ring_len - 1, kv_hi.at[pl.ds(0, half)]),
            ),
        )
        start_copies(moves, sems)
        wait_copies(moves, sems)
        rows = lax.broadcasted_iota(jnp.int32, (TILE, TILE), 0)

        def lse_of(t):
            tile = first_tile + t
            q_t = q[span(t), :]
            tops, totals = [], []
            for n in range(nbr_count):
                near = nbr[tile * nbr_count + n]
                score = dot(k_ext[span(near - ext_base), :], q_t, NT) * scale_two
                score = jnp.where(rows < cnt[near], score, -jnp.inf)
                peak = jnp.max(score, axis=0, keepdims=True)
                tops.append(peak)
                totals.append(jnp.sum(jnp.exp2(score - peak), axis=0, keepdims=True))
            top = tops[0]
            for peak in tops[1:]:
                top = jnp.maximum(top, peak)
            total = totals[0] * jnp.exp2(tops[0] - top)
            for part, peak in zip(totals[1:], tops[1:]):
                total = total + part * jnp.exp2(peak - top)
            g_t = jnp.where(rows < cnt[tile], g[span(t), :].astype(jnp.float32), 0.0)
            prod = g_t * o[span(t), :].astype(jnp.float32)
            delta = jnp.sum(prod.T, axis=0, keepdims=True)
            return top + jnp.log2(total), delta

        def step(i, carry):
            first = lse_of(2 * i)
            second = lse_of(2 * i + 1)
            for t, (log_row, delta) in ((2 * i, first), (2 * i + 1, second)):
                stat_all[pl.ds(t, 1), :] = log_row
                stat_all[pl.ds(tiles_dev + t, 1), :] = delta
            return carry

        lax.fori_loop(0, tiles_dev // 2, step, 0)
        for side, out in ((0, stat_lo), (1, stat_hi)):
            out[pl.ds(0, half_tiles), :] = stat_all[pl.ds(side * half_tiles, half_tiles), :]
            out[pl.ds(half_tiles, half_tiles), :] = stat_all[
                pl.ds(tiles_dev + side * half_tiles, half_tiles), :
            ]

    return kernel


def grads_kernel(tiles_dev, tiles_all, nbr_count, ring_len, peers):
    half_tiles = tiles_dev // 2
    half = half_tiles * TILE
    own = tiles_dev * TILE
    share = own // peers
    tile_peers = TILE // share
    scale = TILE ** (-0.5)
    scale_two = scale * math.log2(math.e)

    def kernel(
        shard, nbr, cnt, q_any, k_any, v_any, g_any, kv_lo, kv_hi, kz, vz,
        qg_lo, qg_hi, qz, gz, stat_any, slo, shi,
        joint, q, g, k_ext, v_ext, q_near, g_near, dk_acc, dv_acc, stats, stats_near, pairs, sems,
    ):
        s = shard[0]
        first_tile = s * tiles_dev
        ext_base = first_tile - half_tiles
        col = lax.rem(s, ring_len)
        at_low = col == 0
        at_high = col == ring_len - 1
        first_half = pl.ds(0, half)
        second_half = pl.ds(half, half)
        above = pl.ds(half + own, half)
        moves = (
            (k_ext.at[pl.ds(half, own)], (k_any,)),
            (v_ext.at[pl.ds(half, own)], (v_any,)),
            (q, (q_any,)),
            (g, (g_any,)),
            (stats, (stat_any,)),
            (stats_near.at[0], (slo,)),
            (stats_near.at[1], (shi,)),
            (k_ext.at[first_half], (kz, at_low, kv_lo.at[first_half])),
            (k_ext.at[above], (kz, at_high, kv_hi.at[first_half])),
            (v_ext.at[first_half], (vz, at_low, kv_lo.at[second_half])),
            (v_ext.at[above], (vz, at_high, kv_hi.at[second_half])),
            (q_near.at[first_half], (qz, at_low, qg_lo.at[first_half])),
            (q_near.at[second_half], (qz, at_high, qg_hi.at[first_half])),
            (g_near.at[first_half], (gz, at_low, qg_lo.at[second_half])),
            (g_near.at[second_half], (gz, at_high, qg_hi.at[second_half])),
        )
        start_copies(moves, sems)
        zero = jnp.zeros((own, TILE), jnp.float32)
        dk_acc[pl.ds(0, own), :] = zero
        dv_acc[pl.ds(0, own), :] = zero

        def scan(i, count):
            tile = jnp.where(
                i < half_tiles, first_tile - half_tiles + i, first_tile + tiles_dev + i - half_tiles
            )
            inside = (tile >= 0) & (tile < tiles_all)
            safe = jnp.where(inside, tile, 0)
            for n in range(1, nbr_count):
                mine = nbr[safe * nbr_count + n] - first_tile
                hit = inside & (mine >= 0) & (mine < tiles_dev)
                pairs[0, count] = i
                pairs[1, count] = mine
                count = count + hit.astype(jnp.int32)
            return count

        count = lax.fori_loop(0, tiles_dev, scan, jnp.int32(0))
        pairs[0, count] = 0
        pairs[1, count] = tiles_dev
        wait_copies(moves, sems)
        rows = lax.broadcasted_iota(jnp.int32, (TILE, TILE), 0)

        def queries(ref, t, tile):
            g_t = jnp.where(rows < cnt[tile], ref[span(t), :].astype(jnp.float32), 0.0)
            return g_t.astype(jnp.bfloat16)

        def terms(place, held, q_t, g_t, log_row, delta):
            key = k_ext[span(place), :]
            score = dot(key, q_t, NT) * scale_two
            prob = jnp.exp2(jnp.where(rows < held, score - log_row, -jnp.inf))
            dprob = dot(v_ext[span(place), :], g_t, NT)
            dscore = (prob * (dprob - delta) * scale).astype(jnp.bfloat16)
            return key, prob.astype(jnp.bfloat16), dscore

        def own_step(t, carry):
            tile = first_tile + t
            q_t = q[span(t), :]
            g_t = queries(g, t, tile)
            log_row = stats[pl.ds(t, 1), :]
            delta = stats[pl.ds(tiles_dev + t, 1), :]
            places, keys, probs, dscores = [], [], [], []
            for n in range(nbr_count):
                near = nbr[tile * nbr_count + n]
                place = near - ext_base
                mine = place - half_tiles
                places.append(jnp.where((mine >= 0) & (mine < tiles_dev), mine, tiles_dev))
                key, prob, dscore = terms(place, cnt[near], q_t, g_t, log_row, delta)
                keys.append(key)
                probs.append(prob)
                dscores.append(dscore)
            dq = dot(jnp.concatenate(dscores), jnp.concatenate(keys), TN)
            sums = [(dot(ds, q_t, NN), dot(pb, g_t, NN)) for ds, pb in zip(dscores, probs)]
            for mine, (dk, dv) in zip(places, sums):
                dk_acc[span(mine), :] += dk
                dv_acc[span(mine), :] += dv
            joint[pl.ds(t * tile_peers, tile_peers), 0] = (
                dq.astype(jnp.bfloat16).reshape(tile_peers, share, TILE)
            )
            return carry

        lax.fori_loop(0, tiles_dev, own_step, 0)

        def near_terms(index):
            i = pairs[0, index]
            mine = pairs[1, index]
            read = jnp.minimum(mine, tiles_dev - 1)
            side = jnp.where(i < half_tiles, 0, 1)
            line = i - side * half_tiles
            tile = first_tile + jnp.where(side == 0, i - half_tiles, tiles_dev + line)
            q_t = q_near[span(i), :]
            g_t = queries(g_near, i, jnp.clip(tile, 0, tiles_all - 1))
            log_row = stats_near[side, pl.ds(line, 1), :]
            delta = stats_near[side, pl.ds(half_tiles + line, 1), :]
            held = cnt[first_tile + read]
            _, prob, dscore = terms(read + half_tiles, held, q_t, g_t, log_row, delta)
            return mine, dot(dscore, q_t, NN), dot(prob, g_t, NN)

        def near_step(j, carry):
            first = near_terms(2 * j)
            second = near_terms(2 * j + 1)
            for mine, dk, dv in (first, second):
                dk_acc[span(mine), :] += dk
                dv_acc[span(mine), :] += dv
            return carry

        lax.fori_loop(0, (count + 1) // 2, near_step, 0)
        for which, acc in ((1, dk_acc), (2, dv_acc)):
            joint[:, which] = (
                acc[pl.ds(0, own), :].astype(jnp.bfloat16).reshape(peers, share, TILE)
            )

    return kernel


def routes(seq_count, ring_len):
    spots = [divmod(s, ring_len) for s in range(seq_count)]

    def pairs(move):
        out = []
        for s, (r, x) in enumerate(spots):
            to = move(r, x)
            if to is not None and 0 <= to[0] < seq_count // ring_len:
                out.append((s, to[0] * ring_len + to[1]))
        return out

    last = ring_len - 1

    def ends(at_first, at_last):
        return pairs(lambda r, x: at_first(r) if x == 0 else at_last(r) if x == last else None)

    return {
        "forward": [(i, i + 1) for i in range(seq_count - 1)],
        "backward": [(i + 1, i) for i in range(seq_count - 1)],
        "around": pairs(lambda r, x: (r, (x + 1) % ring_len)),
        "around_back": pairs(lambda r, x: (r, (x - 1) % ring_len)),
        "up": pairs(lambda r, x: (r, x + 1) if x < last else None),
        "down": pairs(lambda r, x: (r, x - 1) if x > 0 else None),
        "cross": ends(lambda r: (r - 1, last), lambda r: (r + 1, 0)),
        "far": ends(lambda r: (r + 1, 0), lambda r: (r - 1, last)),
        "inward": ends(lambda r: (r, 1), lambda r: (r, last - 1)),
        "outward": pairs(
            lambda r, x: (r - 1, last) if x == 1 else (r + 1, 0) if x == last - 1 else None
        ),
    }


def device_work(query_rows, key_rows, value_rows, attn_output, out_grad, neighbours, counts):
    seq_rows, batch, width = out_grad.shape
    shard_tokens, _, head_dim = query_rows.shape
    nbr_count = neighbours.shape[1]
    tiles_all = counts.shape[0]
    tiles_dev = shard_tokens // TILE
    half = shard_tokens // 2
    peers = shard_tokens // seq_rows
    ring_len = 4
    route = routes(lax.axis_size("seq"), ring_len)
    shard = lax.axis_index("seq").astype(jnp.int32)
    at_start = lax.rem(shard, ring_len) == 0

    def move(rows, name):
        return lax.ppermute(rows, "seq", route[name])

    def edge(rows):
        return jnp.where(at_start, rows[:half], rows[half:])

    q = query_rows.reshape(shard_tokens, head_dim)
    k = key_rows.reshape(shard_tokens, head_dim)
    v = value_rows.reshape(shard_tokens, head_dim)
    o = attn_output.reshape(shard_tokens, head_dim)
    table = neighbours.reshape(-1)
    sent = out_grad.reshape(seq_rows, peers, head_dim).transpose(1, 0, 2)
    grads = lax.all_to_all(sent, "head", split_axis=0, concat_axis=0, tiled=True)
    grads = grads.reshape(shard_tokens, head_dim)
    kv_low = move(jnp.concatenate([k[half:], v[half:]]), "around")
    kv_high = move(jnp.concatenate([k[:half], v[:half]]), "around_back")
    k_far = move(edge(k), "cross")
    q_side = move(edge(q), "inward")
    v_far = move(jnp.where(at_start, kv_low[half:], kv_high[half:]), "far")
    q_far = move(q_side, "outward")
    g_far = move(edge(grads), "cross")
    qg_low = move(jnp.concatenate([q[half:], grads[half:]]), "up")
    qg_high = move(jnp.concatenate([q[:half], grads[:half]]), "down")

    smem = pl.BlockSpec(memory_space=pltpu.SMEM)
    vmem = pl.BlockSpec(memory_space=pltpu.VMEM)
    hbm = pl.BlockSpec(memory_space=pl.ANY)
    stat = jax.ShapeDtypeStruct((tiles_dev, head_dim), jnp.float32)
    held = pltpu.VMEM((shard_tokens, head_dim), jnp.bfloat16)
    wide = pltpu.VMEM((2 * shard_tokens, head_dim), jnp.bfloat16)
    acc = pltpu.VMEM((shard_tokens + TILE, head_dim), jnp.float32)
    place = shard.reshape(1)
    stat_all, stat_low, stat_high = pl.pallas_call(
        stats_kernel(tiles_dev, nbr_count, ring_len),
        out_shape=(
            jax.ShapeDtypeStruct((2 * tiles_dev, head_dim), jnp.float32), stat, stat,
        ),
        in_specs=[smem] * 3 + [hbm] * 7,
        out_specs=(vmem,) * 3,
        scratch_shapes=[held, held, held, wide, pltpu.SemaphoreType.DMA((6,))],
        name="rowstats",
    )(place, table, counts, q, k, o, grads, kv_low, kv_high, k_far)
    near_low = move(stat_high, "forward")
    near_high = move(stat_low, "backward")
    joint = pl.pallas_call(
        grads_kernel(tiles_dev, tiles_all, nbr_count, ring_len, peers),
        out_shape=jax.ShapeDtypeStruct((peers, 3, seq_rows, head_dim), jnp.bfloat16),
        in_specs=[smem] * 3 + [hbm] * 15,
        out_specs=vmem,
        scratch_shapes=[
            held, held, wide, wide, held, held, acc, acc,
            pltpu.VMEM((2 * tiles_dev, head_dim), jnp.float32),
            pltpu.VMEM((2, tiles_dev, head_dim), jnp.float32),
            pltpu.SMEM((2, tiles_dev * nbr_count), jnp.int32),
            pltpu.SemaphoreType.DMA((15,)),
        ],
        name="gradsum",
    )(
        place, table, counts, q, k, v, grads, kv_low, kv_high, k_far, v_far,
        qg_low, qg_high, q_far, g_far, stat_all, near_low, near_high,
    )
    back = lax.all_to_all(joint, "head", split_axis=0, concat_axis=0, tiled=True)

    def to_rows(block):
        return block.transpose(1, 0, 2).reshape(seq_rows, batch, width)

    return to_rows(back[:, 0]), to_rows(back[:, 1]), to_rows(back[:, 2])


def solution(mesh):
    placed = (
        P("seq", "head", None),
        P("seq", "head", None),
        P("seq", "head", None),
        P("seq", "head", None),
        P(("seq", "head"), None, None),
        P(),
        P(),
    )
    return jax.shard_map(
        device_work,
        mesh=mesh,
        in_specs=placed,
        out_specs=(
            P(("seq", "head"), None, None),
            P(("seq", "head"), None, None),
            P(("seq", "head"), None, None),
        ),
        check_vma=False,
    )
```

```python
import math

import jax
import jax.numpy as jnp
from jax import lax
from jax.experimental import pallas as pl
from jax.experimental.pallas import tpu as pltpu
from jax.sharding import PartitionSpec as P

TILE = 128
NT = (((1,), (1,)), ((), ()))
NN = (((1,), (0,)), ((), ()))
TN = (((0,), (0,)), ((), ()))


def dot(a, b, dims):
    return lax.dot_general(a, b, dims, preferred_element_type=jnp.float32)


def span(t):
    return pl.ds(pl.multiple_of(t * TILE, TILE), TILE)


def start_copies(moves, sems):
    for i, (dst, choice) in enumerate(moves):
        if len(choice) == 1:
            pltpu.make_async_copy(choice[0], dst, sems.at[i]).start()
        else:
            far, use_far, near = choice

            @pl.when(use_far)
            def _():
                pltpu.make_async_copy(far, dst, sems.at[i]).start()

            @pl.when(jnp.logical_not(use_far))
            def _():
                pltpu.make_async_copy(near, dst, sems.at[i]).start()


def wait_copies(moves, sems):
    for i, (dst, choice) in enumerate(moves):
        pltpu.make_async_copy(choice[-1], dst, sems.at[i]).wait()


def stats_kernel(tiles_dev, nbr_count, ring_len):
    half_tiles = tiles_dev // 2
    half = half_tiles * TILE
    own = tiles_dev * TILE
    scale_two = TILE ** (-0.5) * math.log2(math.e)

    def kernel(
        shard, nbr, cnt, q_any, k_any, o_any, g_any, k_lo, k_hi, kz,
        stat_all, stat_lo, stat_hi,
        q, o, g, k_ext, sems,
    ):
        s = shard[0]
        first_tile = s * tiles_dev
        ext_base = first_tile - half_tiles
        col = lax.rem(s, ring_len)
        moves = (
            (k_ext.at[pl.ds(half, own)], (k_any,)),
            (q, (q_any,)),
            (o, (o_any,)),
            (g, (g_any,)),
            (k_ext.at[pl.ds(0, half)], (kz, col == 0, k_lo)),
            (k_ext.at[pl.ds(half + own, half)], (kz, col == ring_len - 1, k_hi)),
        )
        start_copies(moves, sems)
        wait_copies(moves, sems)
        rows = lax.broadcasted_iota(jnp.int32, (TILE, TILE), 0)

        def lse_of(t):
            tile = first_tile + t
            q_t = q[span(t), :]
            tops, totals = [], []
            for n in range(nbr_count):
                near = nbr[tile * nbr_count + n]
                score = dot(k_ext[span(near - ext_base), :], q_t, NT) * scale_two
                score = jnp.where(rows < cnt[near], score, -jnp.inf)
                peak = jnp.max(score, axis=0, keepdims=True)
                tops.append(peak)
                totals.append(jnp.sum(jnp.exp2(score - peak), axis=0, keepdims=True))
            top = tops[0]
            for peak in tops[1:]:
                top = jnp.maximum(top, peak)
            total = totals[0] * jnp.exp2(tops[0] - top)
            for part, peak in zip(totals[1:], tops[1:]):
                total = total + part * jnp.exp2(peak - top)
            g_t = jnp.where(rows < cnt[tile], g[span(t), :].astype(jnp.float32), 0.0)
            prod = g_t * o[span(t), :].astype(jnp.float32)
            delta = jnp.sum(prod.T, axis=0, keepdims=True)
            return top + jnp.log2(total), delta

        def step(i, carry):
            first = lse_of(2 * i)
            second = lse_of(2 * i + 1)
            for t, (log_row, delta) in ((2 * i, first), (2 * i + 1, second)):
                stat_all[pl.ds(t, 1), :] = log_row
                stat_all[pl.ds(tiles_dev + t, 1), :] = delta
            return carry

        lax.fori_loop(0, tiles_dev // 2, step, 0)
        for side, out in ((0, stat_lo), (1, stat_hi)):
            out[pl.ds(0, half_tiles), :] = stat_all[pl.ds(side * half_tiles, half_tiles), :]
            out[pl.ds(half_tiles, half_tiles), :] = stat_all[
                pl.ds(tiles_dev + side * half_tiles, half_tiles), :
            ]

    return kernel


def grads_kernel(tiles_dev, tiles_all, nbr_count, ring_len, peers):
    half_tiles = tiles_dev // 2
    half = half_tiles * TILE
    own = tiles_dev * TILE
    share = own // peers
    tile_peers = TILE // share
    scale = TILE ** (-0.5)
    scale_two = scale * math.log2(math.e)

    def kernel(
        shard, nbr, cnt, q_any, k_any, v_any, g_any, k_lo, k_hi, kz,
        lo, hi, vz, qz, gz, stat_any, slo, shi,
        joint, q, g, k_ext, v_ext, q_near, g_near, dk_acc, dv_acc, stats, stats_near, pairs, sems,
    ):
        s = shard[0]
        first_tile = s * tiles_dev
        ext_base = first_tile - half_tiles
        col = lax.rem(s, ring_len)
        at_low = col == 0
        at_high = col == ring_len - 1
        first_half = pl.ds(0, half)
        second_half = pl.ds(half, half)
        third_half = pl.ds(2 * half, half)
        above = pl.ds(half + own, half)
        moves = (
            (k_ext.at[pl.ds(half, own)], (k_any,)),
            (v_ext.at[pl.ds(half, own)], (v_any,)),
            (q, (q_any,)),
            (g, (g_any,)),
            (stats, (stat_any,)),
            (stats_near.at[0], (slo,)),
            (stats_near.at[1], (shi,)),
            (k_ext.at[first_half], (kz, at_low, k_lo)),
            (k_ext.at[above], (kz, at_high, k_hi)),
            (v_ext.at[first_half], (vz, at_low, lo.at[first_half])),
            (v_ext.at[above], (vz, at_high, hi.at[first_half])),
            (q_near.at[first_half], (qz, at_low, lo.at[second_half])),
            (q_near.at[second_half], (qz, at_high, hi.at[second_half])),
            (g_near.at[first_half], (gz, at_low, lo.at[third_half])),
            (g_near.at[second_half], (gz, at_high, hi.at[third_half])),
        )
        start_copies(moves, sems)
        zero = jnp.zeros((own, TILE), jnp.float32)
        dk_acc[pl.ds(0, own), :] = zero
        dv_acc[pl.ds(0, own), :] = zero

        def scan(i, count):
            tile = jnp.where(
                i < half_tiles, first_tile - half_tiles + i, first_tile + tiles_dev + i - half_tiles
            )
            inside = (tile >= 0) & (tile < tiles_all)
            safe = jnp.where(inside, tile, 0)
            for n in range(1, nbr_count):
                mine = nbr[safe * nbr_count + n] - first_tile
                hit = inside & (mine >= 0) & (mine < tiles_dev)
                pairs[0, count] = i
                pairs[1, count] = mine
                count = count + hit.astype(jnp.int32)
            return count

        count = lax.fori_loop(0, tiles_dev, scan, jnp.int32(0))
        pairs[0, count] = 0
        pairs[1, count] = tiles_dev
        wait_copies(moves, sems)
        rows = lax.broadcasted_iota(jnp.int32, (TILE, TILE), 0)

        def queries(ref, t, tile):
            g_t = jnp.where(rows < cnt[tile], ref[span(t), :].astype(jnp.float32), 0.0)
            return g_t.astype(jnp.bfloat16)

        def terms(place, held, q_t, g_t, log_row, delta):
            key = k_ext[span(place), :]
            score = dot(key, q_t, NT) * scale_two
            prob = jnp.exp2(jnp.where(rows < held, score - log_row, -jnp.inf))
            dprob = dot(v_ext[span(place), :], g_t, NT)
            dscore = (prob * (dprob - delta) * scale).astype(jnp.bfloat16)
            return key, prob.astype(jnp.bfloat16), dscore

        def own_terms(t):
            tile = first_tile + t
            q_t = q[span(t), :]
            g_t = queries(g, t, tile)
            log_row = stats[pl.ds(t, 1), :]
            delta = stats[pl.ds(tiles_dev + t, 1), :]
            places, keys, probs, dscores = [], [], [], []
            for n in range(nbr_count):
                near = nbr[tile * nbr_count + n]
                place = near - ext_base
                mine = place - half_tiles
                places.append(jnp.where((mine >= 0) & (mine < tiles_dev), mine, tiles_dev))
                key, prob, dscore = terms(place, cnt[near], q_t, g_t, log_row, delta)
                keys.append(key)
                probs.append(prob)
                dscores.append(dscore)
            return t, q_t, g_t, places, keys, probs, dscores

        def own_sums(t, q_t, g_t, places, keys, probs, dscores):
            for mine, dscore, prob in zip(places, dscores, probs):
                dk_acc[span(mine), :] += dot(dscore, q_t, NN)
                dv_acc[span(mine), :] += dot(prob, g_t, NN)
            dq = dot(jnp.concatenate(dscores), jnp.concatenate(keys), TN)
            joint[pl.ds(t * tile_peers, tile_peers), 0] = (
                dq.astype(jnp.bfloat16).reshape(tile_peers, share, TILE)
            )

        def own_step(i, carry):
            first = own_terms(2 * i)
            second = own_terms(2 * i + 1)
            own_sums(*first)
            own_sums(*second)
            return carry

        lax.fori_loop(0, tiles_dev // 2, own_step, 0)

        def near_terms(index):
            i = pairs[0, index]
            mine = pairs[1, index]
            read = jnp.minimum(mine, tiles_dev - 1)
            side = jnp.where(i < half_tiles, 0, 1)
            line = i - side * half_tiles
            tile = first_tile + jnp.where(side == 0, i - half_tiles, tiles_dev + line)
            q_t = q_near[span(i), :]
            g_t = queries(g_near, i, jnp.clip(tile, 0, tiles_all - 1))
            log_row = stats_near[side, pl.ds(line, 1), :]
            delta = stats_near[side, pl.ds(half_tiles + line, 1), :]
            held = cnt[first_tile + read]
            _, prob, dscore = terms(read + half_tiles, held, q_t, g_t, log_row, delta)
            return mine, dot(dscore, q_t, NN), dot(prob, g_t, NN)

        def near_step(j, carry):
            first = near_terms(2 * j)
            second = near_terms(2 * j + 1)
            for mine, dk, dv in (first, second):
                dk_acc[span(mine), :] += dk
                dv_acc[span(mine), :] += dv
            return carry

        lax.fori_loop(0, (count + 1) // 2, near_step, 0)
        for which, acc in ((1, dk_acc), (2, dv_acc)):
            joint[:, which] = (
                acc[pl.ds(0, own), :].astype(jnp.bfloat16).reshape(peers, share, TILE)
            )

    return kernel


def routes(seq_count, ring_len):
    spots = [divmod(s, ring_len) for s in range(seq_count)]

    def pairs(move):
        out = []
        for s, (r, x) in enumerate(spots):
            to = move(r, x)
            if to is not None and 0 <= to[0] < seq_count // ring_len:
                out.append((s, to[0] * ring_len + to[1]))
        return out

    last = ring_len - 1

    def ends(at_first, at_last):
        return pairs(lambda r, x: at_first(r) if x == 0 else at_last(r) if x == last else None)

    return {
        "forward": [(i, i + 1) for i in range(seq_count - 1)],
        "backward": [(i + 1, i) for i in range(seq_count - 1)],
        "around": pairs(lambda r, x: (r, (x + 1) % ring_len)),
        "around_back": pairs(lambda r, x: (r, (x - 1) % ring_len)),
        "up": pairs(lambda r, x: (r, x + 1) if x < last else None),
        "down": pairs(lambda r, x: (r, x - 1) if x > 0 else None),
        "cross": ends(lambda r: (r - 1, last), lambda r: (r + 1, 0)),
        "far": ends(lambda r: (r + 1, 0), lambda r: (r - 1, last)),
        "inward": ends(lambda r: (r, 1), lambda r: (r, last - 1)),
        "inward_two": ends(lambda r: (r, last - 1), lambda r: (r, 1)),
        "outward_two": pairs(
            lambda r, x: (r + 1, 0) if x == 1 else (r - 1, last) if x == last - 1 else None
        ),
        "outward": pairs(
            lambda r, x: (r - 1, last) if x == 1 else (r + 1, 0) if x == last - 1 else None
        ),
    }


def device_work(query_rows, key_rows, value_rows, attn_output, out_grad, neighbours, counts):
    seq_rows, batch, width = out_grad.shape
    shard_tokens, _, head_dim = query_rows.shape
    nbr_count = neighbours.shape[1]
    tiles_all = counts.shape[0]
    tiles_dev = shard_tokens // TILE
    half = shard_tokens // 2
    peers = shard_tokens // seq_rows
    ring_len = 4
    route = routes(lax.axis_size("seq"), ring_len)
    shard = lax.axis_index("seq").astype(jnp.int32)
    at_start = lax.rem(shard, ring_len) == 0

    def move(rows, name):
        return lax.ppermute(rows, "seq", route[name])

    def edge(rows):
        return jnp.where(at_start, rows[:half], rows[half:])

    q = query_rows.reshape(shard_tokens, head_dim)
    k = key_rows.reshape(shard_tokens, head_dim)
    v = value_rows.reshape(shard_tokens, head_dim)
    o = attn_output.reshape(shard_tokens, head_dim)
    table = neighbours.reshape(-1)
    sent = out_grad.reshape(seq_rows, peers, head_dim).transpose(1, 0, 2)
    grads = lax.all_to_all(sent, "head", split_axis=0, concat_axis=0, tiled=True)
    grads = grads.reshape(shard_tokens, head_dim)
    k_low = move(k[half:], "around")
    k_high = move(k[:half], "around_back")
    q_side = move(edge(q), "inward")
    v_side = move(edge(v), "inward_two")
    k_far = move(jnp.where(at_start, k_low, k_high), "far")
    q_far = move(q_side, "outward")
    v_far = move(v_side, "outward_two")
    g_far = move(edge(grads), "cross")
    low = move(jnp.concatenate([v[half:], q[half:], grads[half:]]), "up")
    high = move(jnp.concatenate([v[:half], q[:half], grads[:half]]), "down")

    smem = pl.BlockSpec(memory_space=pltpu.SMEM)
    vmem = pl.BlockSpec(memory_space=pltpu.VMEM)
    hbm = pl.BlockSpec(memory_space=pl.ANY)
    stat = jax.ShapeDtypeStruct((tiles_dev, head_dim), jnp.float32)
    held = pltpu.VMEM((shard_tokens, head_dim), jnp.bfloat16)
    wide = pltpu.VMEM((2 * shard_tokens, head_dim), jnp.bfloat16)
    acc = pltpu.VMEM((shard_tokens + TILE, head_dim), jnp.float32)
    place = shard.reshape(1)
    stat_all, stat_low, stat_high = pl.pallas_call(
        stats_kernel(tiles_dev, nbr_count, ring_len),
        out_shape=(
            jax.ShapeDtypeStruct((2 * tiles_dev, head_dim), jnp.float32), stat, stat,
        ),
        in_specs=[smem] * 3 + [hbm] * 7,
        out_specs=(vmem,) * 3,
        scratch_shapes=[held, held, held, wide, pltpu.SemaphoreType.DMA((6,))],
        name="rowstats",
    )(place, table, counts, q, k, o, grads, k_low, k_high, k_far)
    near_low = move(stat_high, "forward")
    near_high = move(stat_low, "backward")
    joint = pl.pallas_call(
        grads_kernel(tiles_dev, tiles_all, nbr_count, ring_len, peers),
        out_shape=jax.ShapeDtypeStruct((peers, 3, seq_rows, head_dim), jnp.bfloat16),
        in_specs=[smem] * 3 + [hbm] * 15,
        out_specs=vmem,
        scratch_shapes=[
            held, held, wide, wide, held, held, acc, acc,
            pltpu.VMEM((2 * tiles_dev, head_dim), jnp.float32),
            pltpu.VMEM((2, tiles_dev, head_dim), jnp.float32),
            pltpu.SMEM((2, tiles_dev * nbr_count), jnp.int32),
            pltpu.SemaphoreType.DMA((15,)),
        ],
        name="gradsum",
    )(
        place, table, counts, q, k, v, grads, k_low, k_high, k_far,
        low, high, v_far, q_far, g_far, stat_all, near_low, near_high,
    )
    back = lax.all_to_all(joint, "head", split_axis=0, concat_axis=0, tiled=True)

    def to_rows(block):
        return block.transpose(1, 0, 2).reshape(seq_rows, batch, width)

    return to_rows(back[:, 0]), to_rows(back[:, 1]), to_rows(back[:, 2])


def solution(mesh):
    placed = (
        P("seq", "head", None),
        P("seq", "head", None),
        P("seq", "head", None),
        P("seq", "head", None),
        P(("seq", "head"), None, None),
        P(),
        P(),
    )
    return jax.shard_map(
        device_work,
        mesh=mesh,
        in_specs=placed,
        out_specs=(
            P(("seq", "head"), None, None),
            P(("seq", "head"), None, None),
            P(("seq", "head"), None, None),
        ),
        check_vma=False,
    )
```

```python
import math

import jax
import jax.numpy as jnp
from jax import lax
from jax.experimental import pallas as pl
from jax.experimental.pallas import tpu as pltpu
from jax.sharding import PartitionSpec as P

TILE = 128
NT = (((1,), (1,)), ((), ()))
NN = (((1,), (0,)), ((), ()))
TN = (((0,), (0,)), ((), ()))


def dot(a, b, dims):
    return lax.dot_general(a, b, dims, preferred_element_type=jnp.float32)


def span(t):
    return pl.ds(pl.multiple_of(t * TILE, TILE), TILE)


def start_copies(moves, sems):
    for i, (dst, choice) in enumerate(moves):
        if len(choice) == 1:
            pltpu.make_async_copy(choice[0], dst, sems.at[i]).start()
        else:
            far, use_far, near = choice

            @pl.when(use_far)
            def _():
                pltpu.make_async_copy(far, dst, sems.at[i]).start()

            @pl.when(jnp.logical_not(use_far))
            def _():
                pltpu.make_async_copy(near, dst, sems.at[i]).start()


def wait_copies(moves, sems):
    for i, (dst, choice) in enumerate(moves):
        pltpu.make_async_copy(choice[-1], dst, sems.at[i]).wait()


def stats_kernel(tiles_dev, nbr_count, ring_len):
    half_tiles = tiles_dev // 2
    half = half_tiles * TILE
    own = tiles_dev * TILE
    scale_two = TILE ** (-0.5) * math.log2(math.e)

    def kernel(
        shard, nbr, cnt, q_any, k_any, o_any, g_any, kv_lo, kv_hi, kz,
        stat_all, stat_lo, stat_hi,
        q, o, g, k_ext, sems,
    ):
        s = shard[0]
        first_tile = s * tiles_dev
        ext_base = first_tile - half_tiles
        col = lax.rem(s, ring_len)
        moves = (
            (k_ext.at[pl.ds(half, own)], (k_any,)),
            (q, (q_any,)),
            (o, (o_any,)),
            (g, (g_any,)),
            (k_ext.at[pl.ds(0, half)], (kz, col == 0, kv_lo.at[pl.ds(0, half)])),
            (
                k_ext.at[pl.ds(half + own, half)],
                (kz, col == ring_len - 1, kv_hi.at[pl.ds(0, half)]),
            ),
        )
        start_copies(moves, sems)
        wait_copies(moves, sems)
        rows = lax.broadcasted_iota(jnp.int32, (TILE, TILE), 0)

        def lse_of(t):
            tile = first_tile + t
            q_t = q[span(t), :]
            tops, totals = [], []
            for n in range(nbr_count):
                near = nbr[tile * nbr_count + n]
                score = dot(k_ext[span(near - ext_base), :], q_t, NT) * scale_two
                score = jnp.where(rows < cnt[near], score, -jnp.inf)
                peak = jnp.max(score, axis=0, keepdims=True)
                tops.append(peak)
                totals.append(jnp.sum(jnp.exp2(score - peak), axis=0, keepdims=True))
            top = tops[0]
            for peak in tops[1:]:
                top = jnp.maximum(top, peak)
            total = totals[0] * jnp.exp2(tops[0] - top)
            for part, peak in zip(totals[1:], tops[1:]):
                total = total + part * jnp.exp2(peak - top)
            g_t = jnp.where(rows < cnt[tile], g[span(t), :].astype(jnp.float32), 0.0)
            prod = g_t * o[span(t), :].astype(jnp.float32)
            delta = jnp.sum(prod.T, axis=0, keepdims=True)
            return top + jnp.log2(total), delta

        def step(i, carry):
            first = lse_of(2 * i)
            second = lse_of(2 * i + 1)
            for t, (log_row, delta) in ((2 * i, first), (2 * i + 1, second)):
                stat_all[pl.ds(t, 1), :] = log_row
                stat_all[pl.ds(tiles_dev + t, 1), :] = delta
            return carry

        lax.fori_loop(0, tiles_dev // 2, step, 0)
        for side, out in ((0, stat_lo), (1, stat_hi)):
            out[pl.ds(0, half_tiles), :] = stat_all[pl.ds(side * half_tiles, half_tiles), :]
            out[pl.ds(half_tiles, half_tiles), :] = stat_all[
                pl.ds(tiles_dev + side * half_tiles, half_tiles), :
            ]

    return kernel


def masked(ref, t, held):
    rows = lax.broadcasted_iota(jnp.int32, (TILE, TILE), 0)
    kept = jnp.where(rows < held, ref[span(t), :].astype(jnp.float32), 0.0)
    return kept.astype(jnp.bfloat16)


def pair_terms(key, value, held, q_t, g_t, log_row, delta):
    rows = lax.broadcasted_iota(jnp.int32, (TILE, TILE), 0)
    scale = TILE ** (-0.5)
    score = dot(key, q_t, NT) * (scale * math.log2(math.e))
    prob = jnp.exp2(jnp.where(rows < held, score - log_row, -jnp.inf))
    dprob = dot(value, g_t, NT)
    dscore = (prob * (dprob - delta) * scale).astype(jnp.bfloat16)
    return prob.astype(jnp.bfloat16), dscore


def own_kernel(tiles_dev, nbr_count, ring_len, peers):
    half_tiles = tiles_dev // 2
    half = half_tiles * TILE
    own = tiles_dev * TILE
    share = own // peers
    tile_peers = TILE // share

    def kernel(
        shard, nbr, cnt, q_any, k_any, v_any, g_any, kv_lo, kv_hi, kz, vz, stat_any,
        dq_ref, dk_ref, dv_ref, q, g, k_ext, v_ext, dk_acc, dv_acc, stats, sems,
    ):
        s = shard[0]
        first_tile = s * tiles_dev
        ext_base = first_tile - half_tiles
        col = lax.rem(s, ring_len)
        at_low = col == 0
        at_high = col == ring_len - 1
        first_half = pl.ds(0, half)
        second_half = pl.ds(half, half)
        above = pl.ds(half + own, half)
        moves = (
            (k_ext.at[pl.ds(half, own)], (k_any,)),
            (v_ext.at[pl.ds(half, own)], (v_any,)),
            (q, (q_any,)),
            (g, (g_any,)),
            (stats, (stat_any,)),
            (k_ext.at[first_half], (kz, at_low, kv_lo.at[first_half])),
            (k_ext.at[above], (kz, at_high, kv_hi.at[first_half])),
            (v_ext.at[first_half], (vz, at_low, kv_lo.at[second_half])),
            (v_ext.at[above], (vz, at_high, kv_hi.at[second_half])),
        )
        start_copies(moves, sems)
        zero = jnp.zeros((own, TILE), jnp.float32)
        dk_acc[pl.ds(0, own), :] = zero
        dv_acc[pl.ds(0, own), :] = zero
        wait_copies(moves, sems)

        def own_terms(t):
            tile = first_tile + t
            q_t = q[span(t), :]
            g_t = masked(g, t, cnt[tile])
            log_row = stats[pl.ds(t, 1), :]
            delta = stats[pl.ds(tiles_dev + t, 1), :]
            places, keys, probs, dscores = [], [], [], []
            for n in range(nbr_count):
                near = nbr[tile * nbr_count + n]
                place = near - ext_base
                mine = place - half_tiles
                places.append(jnp.where((mine >= 0) & (mine < tiles_dev), mine, tiles_dev))
                key = k_ext[span(place), :]
                prob, dscore = pair_terms(
                    key, v_ext[span(place), :], cnt[near], q_t, g_t, log_row, delta
                )
                keys.append(key)
                probs.append(prob)
                dscores.append(dscore)
            return t, q_t, g_t, places, keys, probs, dscores

        def own_sums(t, q_t, g_t, places, keys, probs, dscores):
            for mine, dscore, prob in zip(places, dscores, probs):
                dk_acc[span(mine), :] += dot(dscore, q_t, NN)
                dv_acc[span(mine), :] += dot(prob, g_t, NN)
            dq = dot(jnp.concatenate(dscores), jnp.concatenate(keys), TN)
            dq_ref[pl.ds(t * tile_peers, tile_peers)] = (
                dq.astype(jnp.bfloat16).reshape(tile_peers, share, TILE)
            )

        def own_step(i, carry):
            first = own_terms(2 * i)
            second = own_terms(2 * i + 1)
            own_sums(*first)
            own_sums(*second)
            return carry

        lax.fori_loop(0, tiles_dev // 2, own_step, 0)
        dk_ref[...] = dk_acc[pl.ds(0, own), :]
        dv_ref[...] = dv_acc[pl.ds(0, own), :]

    return kernel


def near_kernel(tiles_dev, tiles_all, nbr_count, ring_len, peers):
    half_tiles = tiles_dev // 2
    half = half_tiles * TILE
    own = tiles_dev * TILE
    share = own // peers

    def kernel(
        shard, nbr, cnt, k_any, v_any, kvq_lo, kvq_hi, qz, glo, ghi, gz, slo, shi, dq_any, dk_any, dv_any,
        joint, k, v, q_near, g_near, dk_acc, dv_acc, stats_near, pairs, sems,
    ):
        s = shard[0]
        first_tile = s * tiles_dev
        col = lax.rem(s, ring_len)
        at_low = col == 0
        at_high = col == ring_len - 1
        first_half = pl.ds(0, half)
        second_half = pl.ds(half, half)
        third_half = pl.ds(2 * half, half)
        moves = (
            (k, (k_any,)),
            (v, (v_any,)),
            (dk_acc.at[pl.ds(0, own)], (dk_any,)),
            (dv_acc.at[pl.ds(0, own)], (dv_any,)),
            (stats_near.at[0], (slo,)),
            (stats_near.at[1], (shi,)),
            (q_near.at[first_half], (qz, at_low, kvq_lo.at[third_half])),
            (q_near.at[second_half], (qz, at_high, kvq_hi.at[third_half])),
            (g_near.at[first_half], (gz, at_low, glo)),
            (g_near.at[second_half], (gz, at_high, ghi)),
            (joint.at[:, 0], (dq_any,)),
        )
        start_copies(moves, sems)

        def scan(i, count):
            tile = jnp.where(
                i < half_tiles, first_tile - half_tiles + i, first_tile + tiles_dev + i - half_tiles
            )
            inside = (tile >= 0) & (tile < tiles_all)
            safe = jnp.where(inside, tile, 0)
            for n in range(1, nbr_count):
                mine = nbr[safe * nbr_count + n] - first_tile
                hit = inside & (mine >= 0) & (mine < tiles_dev)
                pairs[0, count] = i
                pairs[1, count] = mine
                count = count + hit.astype(jnp.int32)
            return count

        count = lax.fori_loop(0, tiles_dev, scan, jnp.int32(0))
        pairs[0, count] = 0
        pairs[1, count] = tiles_dev
        wait_copies(moves, sems)

        def near_terms(index):
            i = pairs[0, index]
            mine = pairs[1, index]
            read = jnp.minimum(mine, tiles_dev - 1)
            side = jnp.where(i < half_tiles, 0, 1)
            line = i - side * half_tiles
            tile = first_tile + jnp.where(side == 0, i - half_tiles, tiles_dev + line)
            q_t = q_near[span(i), :]
            g_t = masked(g_near, i, cnt[jnp.clip(tile, 0, tiles_all - 1)])
            log_row = stats_near[side, pl.ds(line, 1), :]
            delta = stats_near[side, pl.ds(half_tiles + line, 1), :]
            held = cnt[first_tile + read]
            prob, dscore = pair_terms(k[span(read), :], v[span(read), :], held, q_t, g_t, log_row, delta)
            return mine, dot(dscore, q_t, NN), dot(prob, g_t, NN)

        def near_step(j, carry):
            first = near_terms(2 * j)
            second = near_terms(2 * j + 1)
            for mine, dk, dv in (first, second):
                dk_acc[span(mine), :] += dk
                dv_acc[span(mine), :] += dv
            return carry

        lax.fori_loop(0, (count + 1) // 2, near_step, 0)
        for which, acc in ((1, dk_acc), (2, dv_acc)):
            joint[:, which] = (
                acc[pl.ds(0, own), :].astype(jnp.bfloat16).reshape(peers, share, TILE)
            )

    return kernel


def routes(seq_count, ring_len):
    spots = [divmod(s, ring_len) for s in range(seq_count)]

    def pairs(move):
        out = []
        for s, (r, x) in enumerate(spots):
            to = move(r, x)
            if to is not None and 0 <= to[0] < seq_count // ring_len:
                out.append((s, to[0] * ring_len + to[1]))
        return out

    last = ring_len - 1

    def ends(at_first, at_last):
        return pairs(lambda r, x: at_first(r) if x == 0 else at_last(r) if x == last else None)

    return {
        "forward": [(i, i + 1) for i in range(seq_count - 1)],
        "backward": [(i + 1, i) for i in range(seq_count - 1)],
        "around": pairs(lambda r, x: (r, (x + 1) % ring_len)),
        "around_back": pairs(lambda r, x: (r, (x - 1) % ring_len)),
        "up": pairs(lambda r, x: (r, x + 1) if x < last else None),
        "down": pairs(lambda r, x: (r, x - 1) if x > 0 else None),
        "cross": ends(lambda r: (r - 1, last), lambda r: (r + 1, 0)),
        "far": ends(lambda r: (r + 1, 0), lambda r: (r - 1, last)),
        "inward": ends(lambda r: (r, 1), lambda r: (r, last - 1)),
        "inward_two": ends(lambda r: (r, last - 1), lambda r: (r, 1)),
        "outward_two": pairs(
            lambda r, x: (r + 1, 0) if x == 1 else (r - 1, last) if x == last - 1 else None
        ),
        "outward": pairs(
            lambda r, x: (r - 1, last) if x == 1 else (r + 1, 0) if x == last - 1 else None
        ),
    }


def device_work(query_rows, key_rows, value_rows, attn_output, out_grad, neighbours, counts):
    seq_rows, batch, width = out_grad.shape
    shard_tokens, _, head_dim = query_rows.shape
    nbr_count = neighbours.shape[1]
    tiles_all = counts.shape[0]
    tiles_dev = shard_tokens // TILE
    half = shard_tokens // 2
    peers = shard_tokens // seq_rows
    ring_len = 4
    route = routes(lax.axis_size("seq"), ring_len)
    shard = lax.axis_index("seq").astype(jnp.int32)
    at_start = lax.rem(shard, ring_len) == 0

    def move(rows, name):
        return lax.ppermute(rows, "seq", route[name])

    def edge(rows):
        return jnp.where(at_start, rows[:half], rows[half:])

    q = query_rows.reshape(shard_tokens, head_dim)
    k = key_rows.reshape(shard_tokens, head_dim)
    v = value_rows.reshape(shard_tokens, head_dim)
    o = attn_output.reshape(shard_tokens, head_dim)
    table = neighbours.reshape(-1)
    k_side = move(edge(k), "inward")
    v_side = move(edge(v), "inward_two")
    kvq_low = move(jnp.concatenate([k[half:], v[half:], q[half:]]), "around")
    kvq_high = move(jnp.concatenate([k[:half], v[:half], q[:half]]), "around_back")
    sent = out_grad.reshape(seq_rows, peers, head_dim).transpose(1, 0, 2)
    grads = lax.all_to_all(sent, "head", split_axis=0, concat_axis=0, tiled=True)
    grads = grads.reshape(shard_tokens, head_dim)
    k_far = move(k_side, "outward")
    v_far = move(v_side, "outward_two")
    q_low, q_high, grads = lax.optimization_barrier((kvq_low, kvq_high, grads))
    q_far = move(jnp.where(at_start, q_low[2 * half :], q_high[2 * half :]), "far")
    g_far = move(edge(grads), "cross")
    g_low = move(grads[half:], "up")
    g_high = move(grads[:half], "down")

    smem = pl.BlockSpec(memory_space=pltpu.SMEM)
    vmem = pl.BlockSpec(memory_space=pltpu.VMEM)
    hbm = pl.BlockSpec(memory_space=pl.ANY)
    stat = jax.ShapeDtypeStruct((tiles_dev, head_dim), jnp.float32)
    held = pltpu.VMEM((shard_tokens, head_dim), jnp.bfloat16)
    wide = pltpu.VMEM((2 * shard_tokens, head_dim), jnp.bfloat16)
    acc = pltpu.VMEM((shard_tokens + TILE, head_dim), jnp.float32)
    place = shard.reshape(1)
    stat_all, stat_low, stat_high = pl.pallas_call(
        stats_kernel(tiles_dev, nbr_count, ring_len),
        out_shape=(
            jax.ShapeDtypeStruct((2 * tiles_dev, head_dim), jnp.float32), stat, stat,
        ),
        in_specs=[smem] * 3 + [hbm] * 7,
        out_specs=(vmem,) * 3,
        scratch_shapes=[held, held, held, wide, pltpu.SemaphoreType.DMA((6,))],
        name="rowstats",
    )(place, table, counts, q, k, o, grads, kvq_low, kvq_high, k_far)
    near_low = move(stat_high, "forward")
    near_high = move(stat_low, "backward")
    sums = jax.ShapeDtypeStruct((shard_tokens, head_dim), jnp.float32)
    dq, dk, dv = pl.pallas_call(
        own_kernel(tiles_dev, nbr_count, ring_len, peers),
        out_shape=(
            jax.ShapeDtypeStruct((peers, seq_rows, head_dim), jnp.bfloat16), sums, sums,
        ),
        in_specs=[smem] * 3 + [hbm] * 9,
        out_specs=(vmem,) * 3,
        scratch_shapes=[
            held, held, wide, wide, acc, acc,
            pltpu.VMEM((2 * tiles_dev, head_dim), jnp.float32),
            pltpu.SemaphoreType.DMA((9,)),
        ],
        name="owngrads",
    )(place, table, counts, q, k, v, grads, kvq_low, kvq_high, k_far, v_far, stat_all)
    joint = pl.pallas_call(
        near_kernel(tiles_dev, tiles_all, nbr_count, ring_len, peers),
        out_shape=jax.ShapeDtypeStruct((peers, 3, seq_rows, head_dim), jnp.bfloat16),
        in_specs=[smem] * 3 + [hbm] * 13,
        out_specs=vmem,
        scratch_shapes=[
            held, held, held, held, acc, acc,
            pltpu.VMEM((2, tiles_dev, head_dim), jnp.float32),
            pltpu.SMEM((2, tiles_dev * nbr_count), jnp.int32),
            pltpu.SemaphoreType.DMA((11,)),
        ],
        name="neargrads",
    )(
        place, table, counts, k, v, kvq_low, kvq_high, q_far, g_low, g_high, g_far,
        near_low, near_high, dq, dk, dv,
    )
    back = lax.all_to_all(joint, "head", split_axis=0, concat_axis=0, tiled=True)

    def to_rows(block):
        return block.transpose(1, 0, 2).reshape(seq_rows, batch, width)

    return to_rows(back[:, 0]), to_rows(back[:, 1]), to_rows(back[:, 2])


def solution(mesh):
    placed = (
        P("seq", "head", None),
        P("seq", "head", None),
        P("seq", "head", None),
        P("seq", "head", None),
        P(("seq", "head"), None, None),
        P(),
        P(),
    )
    return jax.shard_map(
        device_work,
        mesh=mesh,
        in_specs=placed,
        out_specs=(
            P(("seq", "head"), None, None),
            P(("seq", "head"), None, None),
            P(("seq", "head"), None, None),
        ),
        check_vma=False,
    )
```

```python
import math

import jax
import jax.numpy as jnp
from jax import lax
from jax.experimental import pallas as pl
from jax.experimental.pallas import tpu as pltpu
from jax.sharding import PartitionSpec as P

TILE = 128
STEP_PAIRS = 2
NT = (((1,), (1,)), ((), ()))
NN = (((1,), (0,)), ((), ()))
TN = (((0,), (0,)), ((), ()))


def dot(a, b, dims):
    return lax.dot_general(a, b, dims, preferred_element_type=jnp.float32)


def span(t):
    return pl.ds(pl.multiple_of(t * TILE, TILE), TILE)


def start_copies(moves, sems):
    for i, (dst, choice) in enumerate(moves):
        if len(choice) == 1:
            pltpu.make_async_copy(choice[0], dst, sems.at[i]).start()
        else:
            far, use_far, near = choice

            @pl.when(use_far)
            def _():
                pltpu.make_async_copy(far, dst, sems.at[i]).start()

            @pl.when(jnp.logical_not(use_far))
            def _():
                pltpu.make_async_copy(near, dst, sems.at[i]).start()


def wait_copies(moves, sems):
    for i, (dst, choice) in enumerate(moves):
        pltpu.make_async_copy(choice[-1], dst, sems.at[i]).wait()


def stats_kernel(tiles_dev, nbr_count, ring_len):
    half_tiles = tiles_dev // 2
    half = half_tiles * TILE
    own = tiles_dev * TILE
    scale_two = TILE ** (-0.5) * math.log2(math.e)

    def kernel(
        shard, nbr, cnt, q_any, k_any, o_any, g_any, kv_lo, kv_hi, kz,
        stat_all, stat_lo, stat_hi,
        q, o, g, k_ext, sems,
    ):
        s = shard[0]
        first_tile = s * tiles_dev
        ext_base = first_tile - half_tiles
        col = lax.rem(s, ring_len)
        moves = (
            (k_ext.at[pl.ds(half, own)], (k_any,)),
            (q, (q_any,)),
            (o, (o_any,)),
            (g, (g_any,)),
            (k_ext.at[pl.ds(0, half)], (kz, col == 0, kv_lo.at[pl.ds(0, half)])),
            (
                k_ext.at[pl.ds(half + own, half)],
                (kz, col == ring_len - 1, kv_hi.at[pl.ds(0, half)]),
            ),
        )
        start_copies(moves, sems)
        wait_copies(moves, sems)
        rows = lax.broadcasted_iota(jnp.int32, (TILE, TILE), 0)

        def lse_of(t):
            tile = first_tile + t
            q_t = q[span(t), :]
            tops, totals = [], []
            for n in range(nbr_count):
                near = nbr[tile * nbr_count + n]
                score = dot(k_ext[span(near - ext_base), :], q_t, NT) * scale_two
                score = jnp.where(rows < cnt[near], score, -jnp.inf)
                peak = jnp.max(score, axis=0, keepdims=True)
                tops.append(peak)
                totals.append(jnp.sum(jnp.exp2(score - peak), axis=0, keepdims=True))
            top = tops[0]
            for peak in tops[1:]:
                top = jnp.maximum(top, peak)
            total = totals[0] * jnp.exp2(tops[0] - top)
            for part, peak in zip(totals[1:], tops[1:]):
                total = total + part * jnp.exp2(peak - top)
            g_t = jnp.where(rows < cnt[tile], g[span(t), :].astype(jnp.float32), 0.0)
            prod = g_t * o[span(t), :].astype(jnp.float32)
            delta = jnp.sum(prod.T, axis=0, keepdims=True)
            return top + jnp.log2(total), delta

        def step(i, carry):
            first = lse_of(2 * i)
            second = lse_of(2 * i + 1)
            for t, (log_row, delta) in ((2 * i, first), (2 * i + 1, second)):
                stat_all[pl.ds(t, 1), :] = log_row
                stat_all[pl.ds(tiles_dev + t, 1), :] = delta
            return carry

        lax.fori_loop(0, tiles_dev // 2, step, 0)
        for side, out in ((0, stat_lo), (1, stat_hi)):
            out[pl.ds(0, half_tiles), :] = stat_all[pl.ds(side * half_tiles, half_tiles), :]
            out[pl.ds(half_tiles, half_tiles), :] = stat_all[
                pl.ds(tiles_dev + side * half_tiles, half_tiles), :
            ]

    return kernel


def masked(ref, t, held):
    rows = lax.broadcasted_iota(jnp.int32, (TILE, TILE), 0)
    kept = jnp.where(rows < held, ref[span(t), :].astype(jnp.float32), 0.0)
    return kept.astype(jnp.bfloat16)


def pair_terms(key, value, held, q_t, g_t, log_row, delta):
    rows = lax.broadcasted_iota(jnp.int32, (TILE, TILE), 0)
    scale = TILE ** (-0.5)
    score = dot(key, q_t, NT) * (scale * math.log2(math.e))
    prob = jnp.exp2(jnp.where(rows < held, score - log_row, -jnp.inf))
    dprob = dot(value, g_t, NT)
    dscore = (prob * (dprob - delta) * scale).astype(jnp.bfloat16)
    return prob.astype(jnp.bfloat16), dscore


def own_kernel(tiles_dev, nbr_count, ring_len, peers):
    half_tiles = tiles_dev // 2
    half = half_tiles * TILE
    own = tiles_dev * TILE
    share = own // peers
    tile_peers = TILE // share

    def kernel(
        shard, nbr, cnt, q_any, k_any, v_any, g_any, kv_lo, kv_hi, kz, vz, stat_any,
        dq_ref, dk_ref, dv_ref, q, g, k_ext, v_ext, dk_acc, dv_acc, stats, sems,
    ):
        s = shard[0]
        first_tile = s * tiles_dev
        ext_base = first_tile - half_tiles
        col = lax.rem(s, ring_len)
        at_low = col == 0
        at_high = col == ring_len - 1
        first_half = pl.ds(0, half)
        second_half = pl.ds(half, half)
        above = pl.ds(half + own, half)
        moves = (
            (k_ext.at[pl.ds(half, own)], (k_any,)),
            (v_ext.at[pl.ds(half, own)], (v_any,)),
            (q, (q_any,)),
            (g, (g_any,)),
            (stats, (stat_any,)),
            (k_ext.at[first_half], (kz, at_low, kv_lo.at[first_half])),
            (k_ext.at[above], (kz, at_high, kv_hi.at[first_half])),
            (v_ext.at[first_half], (vz, at_low, kv_lo.at[second_half])),
            (v_ext.at[above], (vz, at_high, kv_hi.at[second_half])),
        )
        start_copies(moves, sems)
        zero = jnp.zeros((own, TILE), jnp.float32)
        dk_acc[pl.ds(0, own), :] = zero
        dv_acc[pl.ds(0, own), :] = zero
        wait_copies(moves, sems)

        def own_terms(t):
            tile = first_tile + t
            q_t = q[span(t), :]
            g_t = masked(g, t, cnt[tile])
            log_row = stats[pl.ds(t, 1), :]
            delta = stats[pl.ds(tiles_dev + t, 1), :]
            places, keys, probs, dscores = [], [], [], []
            for n in range(nbr_count):
                near = nbr[tile * nbr_count + n]
                place = near - ext_base
                mine = place - half_tiles
                places.append(jnp.where((mine >= 0) & (mine < tiles_dev), mine, tiles_dev))
                key = k_ext[span(place), :]
                prob, dscore = pair_terms(
                    key, v_ext[span(place), :], cnt[near], q_t, g_t, log_row, delta
                )
                keys.append(key)
                probs.append(prob)
                dscores.append(dscore)
            return t, q_t, g_t, places, keys, probs, dscores

        def own_sums(t, q_t, g_t, places, keys, probs, dscores):
            for mine, dscore, prob in zip(places, dscores, probs):
                dk_acc[span(mine), :] += dot(dscore, q_t, NN)
                dv_acc[span(mine), :] += dot(prob, g_t, NN)
            dq = dot(jnp.concatenate(dscores), jnp.concatenate(keys), TN)
            dq_ref[pl.ds(t * tile_peers, tile_peers)] = (
                dq.astype(jnp.bfloat16).reshape(tile_peers, share, TILE)
            )

        def own_step(i, carry):
            first = own_terms(2 * i)
            second = own_terms(2 * i + 1)
            own_sums(*first)
            own_sums(*second)
            return carry

        lax.fori_loop(0, tiles_dev // 2, own_step, 0)
        dk_ref[...] = dk_acc[pl.ds(0, own), :]
        dv_ref[...] = dv_acc[pl.ds(0, own), :]

    return kernel


def near_kernel(tiles_dev, tiles_all, nbr_count, ring_len, peers):
    half_tiles = tiles_dev // 2
    half = half_tiles * TILE
    own = tiles_dev * TILE
    share = own // peers

    def kernel(
        shard, nbr, cnt, k_any, v_any, qlo, qhi, qz, glo, ghi, gz, slo, shi, dq_any, dk_any, dv_any,
        joint, k, v, q_near, g_near, dk_acc, dv_acc, stats_near, pairs, sems,
    ):
        s = shard[0]
        first_tile = s * tiles_dev
        col = lax.rem(s, ring_len)
        at_low = col == 0
        at_high = col == ring_len - 1
        first_half = pl.ds(0, half)
        second_half = pl.ds(half, half)
        moves = (
            (k, (k_any,)),
            (v, (v_any,)),
            (dk_acc.at[pl.ds(0, own)], (dk_any,)),
            (dv_acc.at[pl.ds(0, own)], (dv_any,)),
            (stats_near.at[0], (slo,)),
            (stats_near.at[1], (shi,)),
            (q_near.at[first_half], (qz, at_low, qlo)),
            (q_near.at[second_half], (qz, at_high, qhi)),
            (g_near.at[first_half], (gz, at_low, glo)),
            (g_near.at[second_half], (gz, at_high, ghi)),
            (joint.at[:, 0], (dq_any,)),
        )
        start_copies(moves, sems)

        def scan(i, count):
            tile = jnp.where(
                i < half_tiles, first_tile - half_tiles + i, first_tile + tiles_dev + i - half_tiles
            )
            inside = (tile >= 0) & (tile < tiles_all)
            safe = jnp.where(inside, tile, 0)
            for n in range(1, nbr_count):
                mine = nbr[safe * nbr_count + n] - first_tile
                hit = inside & (mine >= 0) & (mine < tiles_dev)
                pairs[0, count] = i
                pairs[1, count] = mine
                count = count + hit.astype(jnp.int32)
            return count

        count = lax.fori_loop(0, tiles_dev, scan, jnp.int32(0))
        for extra in range(STEP_PAIRS - 1):
            pairs[0, count + extra] = 0
            pairs[1, count + extra] = tiles_dev
        wait_copies(moves, sems)

        def near_terms(index):
            i = pairs[0, index]
            mine = pairs[1, index]
            read = jnp.minimum(mine, tiles_dev - 1)
            side = jnp.where(i < half_tiles, 0, 1)
            line = i - side * half_tiles
            tile = first_tile + jnp.where(side == 0, i - half_tiles, tiles_dev + line)
            q_t = q_near[span(i), :]
            g_t = masked(g_near, i, cnt[jnp.clip(tile, 0, tiles_all - 1)])
            log_row = stats_near[side, pl.ds(line, 1), :]
            delta = stats_near[side, pl.ds(half_tiles + line, 1), :]
            held = cnt[first_tile + read]
            prob, dscore = pair_terms(k[span(read), :], v[span(read), :], held, q_t, g_t, log_row, delta)
            return mine, dot(dscore, q_t, NN), dot(prob, g_t, NN)

        def near_step(j, carry):
            for mine, dk, dv in [near_terms(STEP_PAIRS * j + i) for i in range(STEP_PAIRS)]:
                dk_acc[span(mine), :] += dk
                dv_acc[span(mine), :] += dv
            return carry

        lax.fori_loop(0, (count + STEP_PAIRS - 1) // STEP_PAIRS, near_step, 0)
        for which, acc in ((1, dk_acc), (2, dv_acc)):
            joint[:, which] = (
                acc[pl.ds(0, own), :].astype(jnp.bfloat16).reshape(peers, share, TILE)
            )

    return kernel


def routes(seq_count, ring_len):
    spots = [divmod(s, ring_len) for s in range(seq_count)]

    def pairs(move):
        out = []
        for s, (r, x) in enumerate(spots):
            to = move(r, x)
            if to is not None and 0 <= to[0] < seq_count // ring_len:
                out.append((s, to[0] * ring_len + to[1]))
        return out

    last = ring_len - 1

    def ends(at_first, at_last):
        return pairs(lambda r, x: at_first(r) if x == 0 else at_last(r) if x == last else None)

    return {
        "forward": [(i, i + 1) for i in range(seq_count - 1)],
        "backward": [(i + 1, i) for i in range(seq_count - 1)],
        "around": pairs(lambda r, x: (r, (x + 1) % ring_len)),
        "around_back": pairs(lambda r, x: (r, (x - 1) % ring_len)),
        "up": pairs(lambda r, x: (r, x + 1) if x < last else None),
        "down": pairs(lambda r, x: (r, x - 1) if x > 0 else None),
        "cross": ends(lambda r: (r - 1, last), lambda r: (r + 1, 0)),
        "far": ends(lambda r: (r + 1, 0), lambda r: (r - 1, last)),
        "inward": ends(lambda r: (r, 1), lambda r: (r, last - 1)),
        "inward_two": ends(lambda r: (r, last - 1), lambda r: (r, 1)),
        "outward_two": pairs(
            lambda r, x: (r + 1, 0) if x == 1 else (r - 1, last) if x == last - 1 else None
        ),
        "outward": pairs(
            lambda r, x: (r - 1, last) if x == 1 else (r + 1, 0) if x == last - 1 else None
        ),
    }


def device_work(query_rows, key_rows, value_rows, attn_output, out_grad, neighbours, counts):
    seq_rows, batch, width = out_grad.shape
    shard_tokens, _, head_dim = query_rows.shape
    nbr_count = neighbours.shape[1]
    tiles_all = counts.shape[0]
    tiles_dev = shard_tokens // TILE
    half = shard_tokens // 2
    peers = shard_tokens // seq_rows
    ring_len = 4
    route = routes(lax.axis_size("seq"), ring_len)
    shard = lax.axis_index("seq").astype(jnp.int32)
    at_start = lax.rem(shard, ring_len) == 0

    def move(rows, name):
        return lax.ppermute(rows, "seq", route[name])

    def edge(rows):
        return jnp.where(at_start, rows[:half], rows[half:])

    q = query_rows.reshape(shard_tokens, head_dim)
    k = key_rows.reshape(shard_tokens, head_dim)
    v = value_rows.reshape(shard_tokens, head_dim)
    o = attn_output.reshape(shard_tokens, head_dim)
    table = neighbours.reshape(-1)
    kv_low = move(jnp.concatenate([k[half:], v[half:]]), "around")
    kv_high = move(jnp.concatenate([k[:half], v[:half]]), "around_back")
    sent = out_grad.reshape(seq_rows, peers, head_dim).transpose(1, 0, 2)
    grads = lax.all_to_all(sent, "head", split_axis=0, concat_axis=0, tiled=True)
    grads = grads.reshape(shard_tokens, head_dim)
    k_far = move(jnp.where(at_start, kv_low[:half], kv_high[:half]), "far")
    v_side = move(edge(v), "inward_two")
    q_side = move(edge(q), "inward")
    v_far = move(v_side, "outward_two")
    q_far = move(q_side, "outward")
    g_far = move(edge(grads), "cross")
    q_low = move(q[half:], "up")
    q_high = move(q[:half], "down")
    g_low = move(grads[half:], "up")
    g_high = move(grads[:half], "down")

    smem = pl.BlockSpec(memory_space=pltpu.SMEM)
    vmem = pl.BlockSpec(memory_space=pltpu.VMEM)
    hbm = pl.BlockSpec(memory_space=pl.ANY)
    stat = jax.ShapeDtypeStruct((tiles_dev, head_dim), jnp.float32)
    held = pltpu.VMEM((shard_tokens, head_dim), jnp.bfloat16)
    wide = pltpu.VMEM((2 * shard_tokens, head_dim), jnp.bfloat16)
    acc = pltpu.VMEM((shard_tokens + TILE, head_dim), jnp.float32)
    place = shard.reshape(1)
    stat_all, stat_low, stat_high = pl.pallas_call(
        stats_kernel(tiles_dev, nbr_count, ring_len),
        out_shape=(
            jax.ShapeDtypeStruct((2 * tiles_dev, head_dim), jnp.float32), stat, stat,
        ),
        in_specs=[smem] * 3 + [hbm] * 7,
        out_specs=(vmem,) * 3,
        scratch_shapes=[held, held, held, wide, pltpu.SemaphoreType.DMA((6,))],
        name="rowstats",
    )(place, table, counts, q, k, o, grads, kv_low, kv_high, k_far)
    near_low = move(stat_high, "forward")
    near_high = move(stat_low, "backward")
    sums = jax.ShapeDtypeStruct((shard_tokens, head_dim), jnp.float32)
    dq, dk, dv = pl.pallas_call(
        own_kernel(tiles_dev, nbr_count, ring_len, peers),
        out_shape=(
            jax.ShapeDtypeStruct((peers, seq_rows, head_dim), jnp.bfloat16), sums, sums,
        ),
        in_specs=[smem] * 3 + [hbm] * 9,
        out_specs=(vmem,) * 3,
        scratch_shapes=[
            held, held, wide, wide, acc, acc,
            pltpu.VMEM((2 * tiles_dev, head_dim), jnp.float32),
            pltpu.SemaphoreType.DMA((9,)),
        ],
        name="owngrads",
    )(place, table, counts, q, k, v, grads, kv_low, kv_high, k_far, v_far, stat_all)
    joint = pl.pallas_call(
        near_kernel(tiles_dev, tiles_all, nbr_count, ring_len, peers),
        out_shape=jax.ShapeDtypeStruct((peers, 3, seq_rows, head_dim), jnp.bfloat16),
        in_specs=[smem] * 3 + [hbm] * 13,
        out_specs=vmem,
        scratch_shapes=[
            held, held, held, held, acc, acc,
            pltpu.VMEM((2, tiles_dev, head_dim), jnp.float32),
            pltpu.SMEM((2, tiles_dev * nbr_count), jnp.int32),
            pltpu.SemaphoreType.DMA((11,)),
        ],
        name="neargrads",
    )(
        place, table, counts, k, v, q_low, q_high, q_far, g_low, g_high, g_far,
        near_low, near_high, dq, dk, dv,
    )
    back = lax.all_to_all(joint, "head", split_axis=0, concat_axis=0, tiled=True)

    def to_rows(block):
        return block.transpose(1, 0, 2).reshape(seq_rows, batch, width)

    return to_rows(back[:, 0]), to_rows(back[:, 1]), to_rows(back[:, 2])


def solution(mesh):
    placed = (
        P("seq", "head", None),
        P("seq", "head", None),
        P("seq", "head", None),
        P("seq", "head", None),
        P(("seq", "head"), None, None),
        P(),
        P(),
    )
    return jax.shard_map(
        device_work,
        mesh=mesh,
        in_specs=placed,
        out_specs=(
            P(("seq", "head"), None, None),
            P(("seq", "head"), None, None),
            P(("seq", "head"), None, None),
        ),
        check_vma=False,
    )
```

```python
import math

import jax
import jax.numpy as jnp
from jax import lax
from jax.experimental import pallas as pl
from jax.experimental.pallas import tpu as pltpu
from jax.sharding import PartitionSpec as P

TILE = 128
NT = (((1,), (1,)), ((), ()))
NN = (((1,), (0,)), ((), ()))
TN = (((0,), (0,)), ((), ()))


def dot(a, b, dims):
    return lax.dot_general(a, b, dims, preferred_element_type=jnp.float32)


def span(t):
    return pl.ds(pl.multiple_of(t * TILE, TILE), TILE)


def start_copies(moves, sems):
    for i, (dst, choice) in enumerate(moves):
        if len(choice) == 1:
            pltpu.make_async_copy(choice[0], dst, sems.at[i]).start()
        else:
            far, use_far, near = choice

            @pl.when(use_far)
            def _():
                pltpu.make_async_copy(far, dst, sems.at[i]).start()

            @pl.when(jnp.logical_not(use_far))
            def _():
                pltpu.make_async_copy(near, dst, sems.at[i]).start()


def wait_copies(moves, sems):
    for i, (dst, choice) in enumerate(moves):
        pltpu.make_async_copy(choice[-1], dst, sems.at[i]).wait()


def stats_kernel(tiles_dev, nbr_count, ring_len):
    half_tiles = tiles_dev // 2
    half = half_tiles * TILE
    own = tiles_dev * TILE
    scale_two = TILE ** (-0.5) * math.log2(math.e)

    def kernel(
        shard, nbr, cnt, q_any, k_any, o_any, g_any, kv_lo, kv_hi, kz,
        stat_all, stat_lo, stat_hi,
        q, o, g, k_ext, sems,
    ):
        s = shard[0]
        first_tile = s * tiles_dev
        ext_base = first_tile - half_tiles
        col = lax.rem(s, ring_len)
        moves = (
            (k_ext.at[pl.ds(half, own)], (k_any,)),
            (q, (q_any,)),
            (o, (o_any,)),
            (g, (g_any,)),
            (k_ext.at[pl.ds(0, half)], (kz, col == 0, kv_lo.at[pl.ds(0, half)])),
            (
                k_ext.at[pl.ds(half + own, half)],
                (kz, col == ring_len - 1, kv_hi.at[pl.ds(0, half)]),
            ),
        )
        start_copies(moves, sems)
        wait_copies(moves, sems)
        rows = lax.broadcasted_iota(jnp.int32, (TILE, TILE), 0)

        def lse_of(t):
            tile = first_tile + t
            q_t = q[span(t), :]
            tops, totals = [], []
            for n in range(nbr_count):
                near = nbr[tile * nbr_count + n]
                score = dot(k_ext[span(near - ext_base), :], q_t, NT) * scale_two
                score = jnp.where(rows < cnt[near], score, -jnp.inf)
                peak = jnp.max(score, axis=0, keepdims=True)
                tops.append(peak)
                totals.append(jnp.sum(jnp.exp2(score - peak), axis=0, keepdims=True))
            top = tops[0]
            for peak in tops[1:]:
                top = jnp.maximum(top, peak)
            total = totals[0] * jnp.exp2(tops[0] - top)
            for part, peak in zip(totals[1:], tops[1:]):
                total = total + part * jnp.exp2(peak - top)
            g_t = jnp.where(rows < cnt[tile], g[span(t), :].astype(jnp.float32), 0.0)
            prod = g_t * o[span(t), :].astype(jnp.float32)
            delta = jnp.sum(prod.T, axis=0, keepdims=True)
            return top + jnp.log2(total), delta

        def step(i, carry):
            first = lse_of(2 * i)
            second = lse_of(2 * i + 1)
            for t, (log_row, delta) in ((2 * i, first), (2 * i + 1, second)):
                stat_all[pl.ds(t, 1), :] = log_row
                stat_all[pl.ds(tiles_dev + t, 1), :] = delta
            return carry

        lax.fori_loop(0, tiles_dev // 2, step, 0)
        for side, out in ((0, stat_lo), (1, stat_hi)):
            out[pl.ds(0, half_tiles), :] = stat_all[pl.ds(side * half_tiles, half_tiles), :]
            out[pl.ds(half_tiles, half_tiles), :] = stat_all[
                pl.ds(tiles_dev + side * half_tiles, half_tiles), :
            ]

    return kernel


def masked(ref, t, held):
    rows = lax.broadcasted_iota(jnp.int32, (TILE, TILE), 0)
    kept = jnp.where(rows < held, ref[span(t), :].astype(jnp.float32), 0.0)
    return kept.astype(jnp.bfloat16)


def pair_terms(key, value, held, q_t, g_t, log_row, delta):
    rows = lax.broadcasted_iota(jnp.int32, (TILE, TILE), 0)
    scale = TILE ** (-0.5)
    score = dot(key, q_t, NT) * (scale * math.log2(math.e))
    prob = jnp.exp2(jnp.where(rows < held, score - log_row, -jnp.inf))
    dprob = dot(value, g_t, NT)
    dscore = (prob * (dprob - delta) * scale).astype(jnp.bfloat16)
    return prob.astype(jnp.bfloat16), dscore


def own_kernel(tiles_dev, nbr_count, ring_len, peers):
    half_tiles = tiles_dev // 2
    half = half_tiles * TILE
    own = tiles_dev * TILE
    share = own // peers
    tile_peers = TILE // share

    def kernel(
        shard, nbr, cnt, q_any, k_any, v_any, g_any, kv_lo, kv_hi, kz, vz, stat_any,
        dq_ref, dk_ref, dv_ref, q, g, k_ext, v_ext, dk_acc, dv_acc, stats, sems,
    ):
        s = shard[0]
        first_tile = s * tiles_dev
        ext_base = first_tile - half_tiles
        col = lax.rem(s, ring_len)
        at_low = col == 0
        at_high = col == ring_len - 1
        first_half = pl.ds(0, half)
        second_half = pl.ds(half, half)
        above = pl.ds(half + own, half)
        moves = (
            (k_ext.at[pl.ds(half, own)], (k_any,)),
            (v_ext.at[pl.ds(half, own)], (v_any,)),
            (q, (q_any,)),
            (g, (g_any,)),
            (stats, (stat_any,)),
            (k_ext.at[first_half], (kz, at_low, kv_lo.at[first_half])),
            (k_ext.at[above], (kz, at_high, kv_hi.at[first_half])),
            (v_ext.at[first_half], (vz, at_low, kv_lo.at[second_half])),
            (v_ext.at[above], (vz, at_high, kv_hi.at[second_half])),
        )
        start_copies(moves, sems)
        zero = jnp.zeros((own, TILE), jnp.float32)
        dk_acc[pl.ds(0, own), :] = zero
        dv_acc[pl.ds(0, own), :] = zero
        wait_copies(moves, sems)

        def own_terms(t):
            tile = first_tile + t
            q_t = q[span(t), :]
            g_t = masked(g, t, cnt[tile])
            log_row = stats[pl.ds(t, 1), :]
            delta = stats[pl.ds(tiles_dev + t, 1), :]
            places, keys, probs, dscores = [], [], [], []
            for n in range(nbr_count):
                near = nbr[tile * nbr_count + n]
                place = near - ext_base
                mine = place - half_tiles
                places.append(jnp.where((mine >= 0) & (mine < tiles_dev), mine, tiles_dev))
                key = k_ext[span(place), :]
                prob, dscore = pair_terms(
                    key, v_ext[span(place), :], cnt[near], q_t, g_t, log_row, delta
                )
                keys.append(key)
                probs.append(prob)
                dscores.append(dscore)
            return t, q_t, g_t, places, keys, probs, dscores

        def own_sums(t, q_t, g_t, places, keys, probs, dscores):
            for mine, dscore, prob in zip(places, dscores, probs):
                dk_acc[span(mine), :] += dot(dscore, q_t, NN)
                dv_acc[span(mine), :] += dot(prob, g_t, NN)
            dq = dot(jnp.concatenate(dscores), jnp.concatenate(keys), TN)
            dq_ref[pl.ds(t * tile_peers, tile_peers)] = (
                dq.astype(jnp.bfloat16).reshape(tile_peers, share, TILE)
            )

        def own_step(i, carry):
            first = own_terms(2 * i)
            second = own_terms(2 * i + 1)
            own_sums(*first)
            own_sums(*second)
            return carry

        lax.fori_loop(0, tiles_dev // 2, own_step, 0)
        dk_ref[...] = dk_acc[pl.ds(0, own), :]
        dv_ref[...] = dv_acc[pl.ds(0, own), :]

    return kernel


def near_kernel(tiles_dev, tiles_all, nbr_count, ring_len, peers):
    half_tiles = tiles_dev // 2
    half = half_tiles * TILE
    own = tiles_dev * TILE
    share = own // peers

    def kernel(
        shard, nbr, cnt, k_any, v_any, qg_lo, qg_hi, qz, gz, slo, shi, dq_any, dk_any, dv_any,
        joint, k, v, q_near, g_near, dk_acc, dv_acc, stats_near, pairs, sems,
    ):
        s = shard[0]
        first_tile = s * tiles_dev
        col = lax.rem(s, ring_len)
        at_low = col == 0
        at_high = col == ring_len - 1
        first_half = pl.ds(0, half)
        second_half = pl.ds(half, half)
        moves = (
            (k, (k_any,)),
            (v, (v_any,)),
            (dk_acc.at[pl.ds(0, own)], (dk_any,)),
            (dv_acc.at[pl.ds(0, own)], (dv_any,)),
            (stats_near.at[0], (slo,)),
            (stats_near.at[1], (shi,)),
            (q_near.at[first_half], (qz, at_low, qg_lo.at[first_half])),
            (q_near.at[second_half], (qz, at_high, qg_hi.at[first_half])),
            (g_near.at[first_half], (gz, at_low, qg_lo.at[second_half])),
            (g_near.at[second_half], (gz, at_high, qg_hi.at[second_half])),
            (joint.at[:, 0], (dq_any,)),
        )
        start_copies(moves, sems)

        def scan(i, count):
            tile = jnp.where(
                i < half_tiles, first_tile - half_tiles + i, first_tile + tiles_dev + i - half_tiles
            )
            inside = (tile >= 0) & (tile < tiles_all)
            safe = jnp.where(inside, tile, 0)
            for n in range(1, nbr_count):
                mine = nbr[safe * nbr_count + n] - first_tile
                hit = inside & (mine >= 0) & (mine < tiles_dev)
                pairs[0, count] = i
                pairs[1, count] = mine
                count = count + hit.astype(jnp.int32)
            return count

        count = lax.fori_loop(0, tiles_dev, scan, jnp.int32(0))
        pairs[0, count] = 0
        pairs[1, count] = tiles_dev
        wait_copies(moves[:-1], sems)

        def near_terms(index):
            i = pairs[0, index]
            mine = pairs[1, index]
            read = jnp.minimum(mine, tiles_dev - 1)
            side = jnp.where(i < half_tiles, 0, 1)
            line = i - side * half_tiles
            tile = first_tile + jnp.where(side == 0, i - half_tiles, tiles_dev + line)
            q_t = q_near[span(i), :]
            g_t = masked(g_near, i, cnt[jnp.clip(tile, 0, tiles_all - 1)])
            log_row = stats_near[side, pl.ds(line, 1), :]
            delta = stats_near[side, pl.ds(half_tiles + line, 1), :]
            held = cnt[first_tile + read]
            prob, dscore = pair_terms(k[span(read), :], v[span(read), :], held, q_t, g_t, log_row, delta)
            return mine, dot(dscore, q_t, NN), dot(prob, g_t, NN)

        def near_step(j, carry):
            first = near_terms(2 * j)
            second = near_terms(2 * j + 1)
            for mine, dk, dv in (first, second):
                dk_acc[span(mine), :] += dk
                dv_acc[span(mine), :] += dv
            return carry

        lax.fori_loop(0, (count + 1) // 2, near_step, 0)
        pltpu.make_async_copy(dq_any, joint.at[:, 0], sems.at[len(moves) - 1]).wait()
        for which, acc in ((1, dk_acc), (2, dv_acc)):
            joint[:, which] = (
                acc[pl.ds(0, own), :].astype(jnp.bfloat16).reshape(peers, share, TILE)
            )

    return kernel


def routes(seq_count, ring_len):
    spots = [divmod(s, ring_len) for s in range(seq_count)]

    def pairs(move):
        out = []
        for s, (r, x) in enumerate(spots):
            to = move(r, x)
            if to is not None and 0 <= to[0] < seq_count // ring_len:
                out.append((s, to[0] * ring_len + to[1]))
        return out

    last = ring_len - 1

    def ends(at_first, at_last):
        return pairs(lambda r, x: at_first(r) if x == 0 else at_last(r) if x == last else None)

    return {
        "forward": [(i, i + 1) for i in range(seq_count - 1)],
        "backward": [(i + 1, i) for i in range(seq_count - 1)],
        "around": pairs(lambda r, x: (r, (x + 1) % ring_len)),
        "around_back": pairs(lambda r, x: (r, (x - 1) % ring_len)),
        "up": pairs(lambda r, x: (r, x + 1) if x < last else None),
        "down": pairs(lambda r, x: (r, x - 1) if x > 0 else None),
        "cross": ends(lambda r: (r - 1, last), lambda r: (r + 1, 0)),
        "far": ends(lambda r: (r + 1, 0), lambda r: (r - 1, last)),
        "inward": ends(lambda r: (r, 1), lambda r: (r, last - 1)),
        "inward_two": ends(lambda r: (r, last - 1), lambda r: (r, 1)),
        "outward_two": pairs(
            lambda r, x: (r + 1, 0) if x == 1 else (r - 1, last) if x == last - 1 else None
        ),
        "outward": pairs(
            lambda r, x: (r - 1, last) if x == 1 else (r + 1, 0) if x == last - 1 else None
        ),
    }


def device_work(query_rows, key_rows, value_rows, attn_output, out_grad, neighbours, counts):
    seq_rows, batch, width = out_grad.shape
    shard_tokens, _, head_dim = query_rows.shape
    nbr_count = neighbours.shape[1]
    tiles_all = counts.shape[0]
    tiles_dev = shard_tokens // TILE
    half = shard_tokens // 2
    peers = shard_tokens // seq_rows
    ring_len = 4
    route = routes(lax.axis_size("seq"), ring_len)
    shard = lax.axis_index("seq").astype(jnp.int32)
    at_start = lax.rem(shard, ring_len) == 0

    def move(rows, name):
        return lax.ppermute(rows, "seq", route[name])

    def edge(rows):
        return jnp.where(at_start, rows[:half], rows[half:])

    q = query_rows.reshape(shard_tokens, head_dim)
    k = key_rows.reshape(shard_tokens, head_dim)
    v = value_rows.reshape(shard_tokens, head_dim)
    o = attn_output.reshape(shard_tokens, head_dim)
    table = neighbours.reshape(-1)
    kv_low = move(jnp.concatenate([k[half:], v[half:]]), "around")
    kv_high = move(jnp.concatenate([k[:half], v[:half]]), "around_back")
    sent = out_grad.reshape(seq_rows, peers, head_dim).transpose(1, 0, 2)
    grads = lax.all_to_all(sent, "head", split_axis=0, concat_axis=0, tiled=True)
    grads = grads.reshape(shard_tokens, head_dim)
    k_far = move(jnp.where(at_start, kv_low[:half], kv_high[:half]), "far")
    v_side = move(edge(v), "inward_two")
    q_side = move(edge(q), "inward")
    v_far = move(v_side, "outward_two")
    q_far = move(q_side, "outward")
    g_far = move(edge(grads), "cross")
    qg_low = move(jnp.concatenate([q[half:], grads[half:]]), "up")
    qg_high = move(jnp.concatenate([q[:half], grads[:half]]), "down")

    smem = pl.BlockSpec(memory_space=pltpu.SMEM)
    vmem = pl.BlockSpec(memory_space=pltpu.VMEM)
    hbm = pl.BlockSpec(memory_space=pl.ANY)
    stat = jax.ShapeDtypeStruct((tiles_dev, head_dim), jnp.float32)
    held = pltpu.VMEM((shard_tokens, head_dim), jnp.bfloat16)
    wide = pltpu.VMEM((2 * shard_tokens, head_dim), jnp.bfloat16)
    acc = pltpu.VMEM((shard_tokens + TILE, head_dim), jnp.float32)
    place = shard.reshape(1)
    stat_all, stat_low, stat_high = pl.pallas_call(
        stats_kernel(tiles_dev, nbr_count, ring_len),
        out_shape=(
            jax.ShapeDtypeStruct((2 * tiles_dev, head_dim), jnp.float32), stat, stat,
        ),
        in_specs=[smem] * 3 + [hbm] * 7,
        out_specs=(vmem,) * 3,
        scratch_shapes=[held, held, held, wide, pltpu.SemaphoreType.DMA((6,))],
        name="rowstats",
    )(place, table, counts, q, k, o, grads, kv_low, kv_high, k_far)
    near_low = move(stat_high, "forward")
    near_high = move(stat_low, "backward")
    sums = jax.ShapeDtypeStruct((shard_tokens, head_dim), jnp.float32)
    dq, dk, dv = pl.pallas_call(
        own_kernel(tiles_dev, nbr_count, ring_len, peers),
        out_shape=(
            jax.ShapeDtypeStruct((peers, seq_rows, head_dim), jnp.bfloat16), sums, sums,
        ),
        in_specs=[smem] * 3 + [hbm] * 9,
        out_specs=(vmem,) * 3,
        scratch_shapes=[
            held, held, wide, wide, acc, acc,
            pltpu.VMEM((2 * tiles_dev, head_dim), jnp.float32),
            pltpu.SemaphoreType.DMA((9,)),
        ],
        name="owngrads",
    )(place, table, counts, q, k, v, grads, kv_low, kv_high, k_far, v_far, stat_all)
    joint = pl.pallas_call(
        near_kernel(tiles_dev, tiles_all, nbr_count, ring_len, peers),
        out_shape=jax.ShapeDtypeStruct((peers, 3, seq_rows, head_dim), jnp.bfloat16),
        in_specs=[smem] * 3 + [hbm] * 11,
        out_specs=vmem,
        scratch_shapes=[
            held, held, held, held, acc, acc,
            pltpu.VMEM((2, tiles_dev, head_dim), jnp.float32),
            pltpu.SMEM((2, tiles_dev * nbr_count), jnp.int32),
            pltpu.SemaphoreType.DMA((11,)),
        ],
        name="neargrads",
    )(
        place, table, counts, k, v, qg_low, qg_high, q_far, g_far,
        near_low, near_high, dq, dk, dv,
    )
    back = lax.all_to_all(joint, "head", split_axis=0, concat_axis=0, tiled=True)

    def to_rows(block):
        return block.transpose(1, 0, 2).reshape(seq_rows, batch, width)

    return to_rows(back[:, 0]), to_rows(back[:, 1]), to_rows(back[:, 2])


def solution(mesh):
    placed = (
        P("seq", "head", None),
        P("seq", "head", None),
        P("seq", "head", None),
        P("seq", "head", None),
        P(("seq", "head"), None, None),
        P(),
        P(),
    )
    return jax.shard_map(
        device_work,
        mesh=mesh,
        in_specs=placed,
        out_specs=(
            P(("seq", "head"), None, None),
            P(("seq", "head"), None, None),
            P(("seq", "head"), None, None),
        ),
        check_vma=False,
    )
```
